256 devices in a mesh: row: 8 (over z_lo, x), col: 32 (over z_hi, y, core).
Axes of the slice: x: 4, y: 4, z: 8 (z_hi: 4, z_lo: 2; z = z_hi * 2 + z_lo), core: 2. Of those that a mesh axis runs over, the one named last changes fastest.
Arguments:
- image_feats: bfloat16 [3, 56, 224, 1024], P(None, 'row', 'col'), may hold values from -80 to 80
- norm_gain: float32 [1024], replicated, may hold values from 0.5 to 1.5
- w_qkv: bfloat16 [1024, 1536], replicated, may hold values from -0.1875 to 0.1875
- rel_bias: float32 [8, 13, 13], replicated, may hold values from -5 to 355
- w_proj: bfloat16 [512, 1024], replicated, may hold values from -0.25 to 0.25
- out_grad: bfloat16 [3, 56, 224, 1024], P(None, 'row', 'col'), may hold values from -6 to 6
Outputs:
- layer_out: bfloat16 [3, 56, 224, 1024], P(None, 'row', 'col')
- feats_grad: bfloat16 [3, 56, 224, 1024], P(None, 'row', 'col')
- qkv_grad: bfloat16 [1024, 1536], replicated
- proj_grad: bfloat16 [512, 1024], replicated
- gain_grad: float32 [1024], replicated
- bias_grad: float32 [8, 13, 13], replicated
The draws below stay inside these ranges and needn't reach their ends.
All inputs are finite; a program needn't handle non-finite values.
Results may differ from the reference program's by a relative error of at most 0.017.
Values may be sent and summed in bfloat16 or wider, within the bound.
No kernel may reach another device: no remote copies, remote signals or barrier semaphores. Data moves between devices by JAX's collectives and lax.ppermute only.
A program may use at most 128 MiB of HBM per device.

```python
import math
import jax
import jax.numpy as jnp
from jax import lax

D = 1024
HEADS = 8
WIN = 7
TILES = 3
E = 512
RB = 13
H = 56
W = 224


def draw_image_feats(key, part):
    key_base = jax.random.fold_in(key, 11)
    key_chan = jax.random.fold_in(key, 12)
    key_tok = jax.random.fold_in(key, 13)
    channel_scale = jnp.exp(jax.random.uniform(key_chan, (D,), jnp.float32, math.log(0.5), math.log(5.0)))
    token_scale = jnp.exp(jax.random.uniform(key_tok, (TILES, H, W, 1), jnp.float32, math.log(0.4), math.log(4.0)))
    base_values = jnp.clip(jax.random.normal(key_base, (TILES, H, W, D), jnp.float32), -4.0, 4.0)
    return (base_values * channel_scale * token_scale).astype(jnp.bfloat16)


def draw_rel_bias(key, part):
    key_base = jax.random.fold_in(key, 21)
    base_values = jnp.clip(jax.random.normal(key_base, (HEADS, RB, RB), jnp.float32), -5.0, 5.0)
    return base_values


def level_of(stream_key, shape, shards, least, top_value):
    def one(dim, shards_of):
        draws = jax.random.uniform(jax.random.fold_in(jax.random.fold_in(stream_key, 6), dim), (shards_of,), jnp.float32, least / len(shards), top_value / len(shards))
        return jnp.repeat(jnp.exp(draws), shape[dim] // shards_of).reshape((-1,) + (1,) * (len(shape) - dim - 1))

    loudness = one(*shards[0])
    for cut in shards[1:]:
        loudness = loudness * one(*cut)
    return loudness


def noise(stream_key, shape, scale, reach, cuts=(), kind=jnp.bfloat16):
    array = jax.random.normal(stream_key, shape, jnp.float32) * scale
    if len(cuts) > 0:
        array = level_of(stream_key, shape, cuts, -0.22, 0.18) * array
    return jnp.clip(array, min=-reach, max=reach).astype(kind)


def setup_inputs(seed: int = 0) -> dict:
    streams_of = jax.random.split(jax.random.key(seed), 7)
    return {
        "image_feats": draw_image_feats(jax.random.fold_in(streams_of[6], 71), 0),
        "norm_gain": jnp.clip(1.0 + 0.1 * jax.random.normal(streams_of[1], (D,), jnp.float32), 0.5, 1.5),
        "w_qkv": noise(streams_of[2], (D, 3 * E), D ** -0.5, 0.1875),
        "rel_bias": draw_rel_bias(jax.random.fold_in(streams_of[6], 71), 0),
        "w_proj": noise(streams_of[4], (E, D), E ** -0.5, 0.25),
        "out_grad": noise(streams_of[5], (TILES, H, W, D), 1.0, 6.0, ((1, 8), (2, 32))),
    }


norm_eps = 1e-05
highest = lax.Precision.HIGHEST

def rounded(values):
    return lax.optimization_barrier(values.astype(jnp.bfloat16)).astype(jnp.float32)

def product(form, left, right):
    return jnp.einsum(form, left.astype(jnp.float32), right.astype(jnp.float32), precision=highest)

def window_table(extent, length, anchor):
    half_win = WIN // 2
    position = anchor + jnp.arange(length, dtype=jnp.int32)
    first_key = jnp.clip(position - half_win, 0, extent - WIN)
    offsets = jnp.arange(WIN, dtype=jnp.int32)
    keys_at = first_key[:, None] + offsets[None, :]
    relative = keys_at - position[:, None] + (WIN - 1)
    return (keys_at, relative)

def bias_window(rel_bias, rel_rows, rel_cols):
    bias_index = jnp.arange(RB, dtype=jnp.int32)
    row_onehot = (rel_rows[:, :, None] == bias_index[None, None, :]).astype(jnp.float32)
    col_onehot = (rel_cols[:, :, None] == bias_index[None, None, :]).astype(jnp.float32)
    block = jnp.einsum('rax,hxy,cly->rchal', row_onehot, rel_bias, col_onehot, precision=highest)
    return (block, row_onehot, col_onehot)

def window_of(source, row_index, col_index):
    return jnp.take(jnp.take(source, row_index, axis=1), col_index, axis=3)

def forward_rows(queries, source_keys, source_values, row_index, col_index, bias_block):
    head_count, head_size = queries.shape[-2:]
    key_window = window_of(source_keys, row_index, col_index)
    window_shape = key_window.shape[:-1] + (head_count, head_size)
    key_window = key_window.reshape(window_shape).astype(jnp.float32)
    value_window = window_of(source_values, row_index, col_index).reshape(window_shape).astype(jnp.float32)
    score_scale = head_size ** (-0.5)
    scores = product('brchd,braclhd->brchal', queries, key_window) * score_scale + bias_block[None]
    row_peak = lax.optimization_barrier(jnp.max(scores, axis=(-2, -1), keepdims=True))
    exp_terms = jnp.exp(scores - row_peak)
    probs_full = exp_terms / lax.optimization_barrier(jnp.sum(exp_terms, axis=(-2, -1), keepdims=True))
    probs_low = rounded(probs_full)
    attended = product('brchal,braclhd->brchd', probs_low, value_window).astype(jnp.bfloat16)
    return (attended, key_window, value_window, probs_full, probs_low)

def scatter_back(slots, source_shape, row_index, col_index):
    flat_slots = slots.reshape(slots.shape[:-2] + (slots.shape[-2] * slots.shape[-1],))
    pullback = jax.vjp(lambda source: window_of(source, row_index, col_index), jnp.zeros(source_shape, jnp.float32))[1]
    return pullback(flat_slots)[0]

def backward_rows(queries, key_window, value_window, probs_full, probs_low, attn_grad, source_shape, row_index, col_index):
    head_size = queries.shape[-1]
    score_scale = head_size ** (-0.5)
    probs_grad = product('brchd,braclhd->brchal', attn_grad, value_window)
    inner_sum = lax.optimization_barrier(jnp.sum(probs_full * probs_grad, axis=(-2, -1), keepdims=True))
    score_grad = probs_full * (probs_grad - inner_sum)
    block_grad = lax.optimization_barrier(jnp.sum(score_grad, axis=0))
    score_low = rounded(score_grad)
    query_grad = (product('brchal,braclhd->brchd', score_low, key_window) * score_scale).astype(jnp.bfloat16)
    key_slots = product('brchal,brchd->braclhd', score_low, queries) * score_scale
    key_grad = scatter_back(key_slots, source_shape, row_index, col_index)
    value_slots = product('brchal,brchd->braclhd', probs_low, attn_grad)
    value_grad = scatter_back(value_slots, source_shape, row_index, col_index)
    return (query_grad, key_grad, value_grad, block_grad)

def reference(image_feats, norm_gain, w_qkv, rel_bias, w_proj, out_grad):
    tile_count, image_height, image_width, model_dim = image_feats.shape
    head_count = rel_bias.shape[0]
    heads_dim = w_proj.shape[0]
    head_size = heads_dim // head_count
    feats_f32 = image_feats.astype(jnp.float32)
    center = lax.optimization_barrier(jnp.mean(feats_f32, axis=-1, keepdims=True))
    deviation = feats_f32 - center
    spread = lax.optimization_barrier(jnp.mean(deviation * deviation, axis=-1, keepdims=True))
    inv_std = lax.rsqrt(spread + norm_eps)
    normal_x = deviation * inv_std
    normed = (normal_x * norm_gain).astype(jnp.bfloat16)
    normed_rows = normed.reshape(-1, model_dim)
    qkv_out = jnp.dot(normed_rows, w_qkv, preferred_element_type=jnp.float32).astype(jnp.bfloat16)
    qkv_out = qkv_out.reshape(tile_count, image_height, image_width, 3 * heads_dim)
    queries = qkv_out[..., :heads_dim].reshape(tile_count, image_height, image_width, head_count, head_size)
    all_keys = qkv_out[..., heads_dim:2 * heads_dim]
    all_values = qkv_out[..., 2 * heads_dim:]
    col_index, col_rel = window_table(image_width, image_width, 0)
    slab_index = jnp.arange(WIN, dtype=jnp.int32)[None, :]

    def row_inputs(row_pos):
        first_key = jnp.clip(row_pos - WIN // 2, 0, image_height - WIN).astype(jnp.int32)
        key_slab = lax.dynamic_slice_in_dim(all_keys, first_key, WIN, axis=1)
        value_slab = lax.dynamic_slice_in_dim(all_values, first_key, WIN, axis=1)
        query_row = lax.dynamic_slice_in_dim(queries, row_pos, 1, axis=1)
        rel_rows = first_key + slab_index - row_pos + (WIN - 1)
        bias_block, row_onehot, col_onehot = bias_window(rel_bias, rel_rows, col_rel)
        return (first_key, key_slab, value_slab, query_row, bias_block, row_onehot, col_onehot)

    def forward_step(row_pos):
        first_key, key_slab, value_slab, query_row, bias_block, row_onehot, col_onehot = row_inputs(row_pos)
        return forward_rows(query_row, key_slab, value_slab, slab_index, col_index, bias_block)[0]
    row_list = jnp.arange(image_height, dtype=jnp.int32)
    attended = jnp.moveaxis(lax.map(forward_step, row_list), 0, 1)
    attended = attended.reshape(tile_count, image_height, image_width, head_count, head_size)
    attended_rows = attended.reshape(-1, heads_dim)
    grad_rows = out_grad.reshape(-1, model_dim)
    layer_out = (feats_f32 + jnp.dot(attended_rows, w_proj, preferred_element_type=jnp.float32).reshape(feats_f32.shape)).astype(jnp.bfloat16)
    attended_grad = jnp.dot(grad_rows, w_proj.T, preferred_element_type=jnp.float32).astype(jnp.bfloat16)
    attended_grad = attended_grad.reshape(tile_count, image_height, image_width, head_count, head_size)
    proj_grad = jnp.dot(attended_rows.T, grad_rows, preferred_element_type=jnp.float32).astype(jnp.bfloat16)

    def backward_step(carry_in, row_pos):
        total_grad, bias_total = carry_in
        first_key, key_slab, value_slab, query_row, bias_block, row_onehot, col_onehot = row_inputs(row_pos)
        attended_row, key_window, value_window, probs_full, probs_low = forward_rows(query_row, key_slab, value_slab, slab_index, col_index, bias_block)
        grad_row = lax.dynamic_slice_in_dim(attended_grad, row_pos, 1, axis=1)
        query_grad, key_grad, value_grad, block_grad = backward_rows(query_row, key_window, value_window, probs_full, probs_low, grad_row, key_slab.shape, slab_index, col_index)
        slab_grad = jnp.concatenate([key_grad, value_grad], axis=-1)
        current = lax.dynamic_slice_in_dim(total_grad, first_key, WIN, axis=1)
        total_grad = lax.dynamic_update_slice_in_dim(total_grad, current + slab_grad, first_key, axis=1)
        bias_total = bias_total + jnp.einsum('rax,rchal,cly->hxy', row_onehot, block_grad, col_onehot, precision=highest)
        return ((total_grad, bias_total), query_grad)
    start_grad = jnp.zeros((tile_count, image_height, image_width, 2 * heads_dim), jnp.float32)
    start_bias = jnp.zeros(rel_bias.shape, jnp.float32)
    (kv_total, bias_grad), query_rows = lax.scan(backward_step, (start_grad, start_bias), row_list)
    query_grad = jnp.moveaxis(query_rows, 0, 1).reshape(-1, heads_dim)
    qkv_grad_rows = jnp.concatenate([query_grad, kv_total.astype(jnp.bfloat16).reshape(-1, 2 * heads_dim)], axis=-1)
    qkv_grad = jnp.dot(normed_rows.T, qkv_grad_rows, preferred_element_type=jnp.float32).astype(jnp.bfloat16)
    normed_grad = jnp.dot(qkv_grad_rows, w_qkv.T, preferred_element_type=jnp.float32).reshape(feats_f32.shape)
    gain_grad = lax.optimization_barrier(jnp.sum(normed_grad * normal_x, axis=(0, 1, 2)))
    scaled = normed_grad * norm_gain
    correction = scaled - lax.optimization_barrier(jnp.mean(scaled, axis=-1, keepdims=True)) - normal_x * lax.optimization_barrier(jnp.mean(scaled * normal_x, axis=-1, keepdims=True))
    feats_grad = (out_grad.astype(jnp.float32) + inv_std * correction).astype(jnp.bfloat16)
    return (layer_out, feats_grad, qkv_grad, proj_grad, gain_grad, bias_grad)
```

```python
import numpy as np
import jax
import jax.numpy as jnp
from jax import lax
from jax.experimental import pallas as pl
from jax.experimental.pallas import tpu as pltpu
from jax.sharding import Mesh
from jax.sharding import PartitionSpec as P

WIN = 7
EPS = 1e-05
BF = jnp.bfloat16
F32 = jnp.float32
INTERPRET = False

SLOTS = {"own": 0, "up": 64, "dn": 96, "lf": 128, "rt": 160, "ul": 192, "ur": 208, "dl": 224, "dr": 240}
PIECES = ("up", "dn", "lf", "rt", "ul", "ur", "dl", "dr")
ROWS = {"up": 24, "dn": 24, "lf": 24, "rt": 24, "ul": 16, "ur": 16, "dl": 16, "dr": 16}
COMES = {"up": (-1, 0), "dn": (1, 0), "lf": (0, -1), "rt": (0, 1), "ul": (-1, -1), "ur": (-1, 1), "dl": (1, -1), "dr": (1, 1)}


def tables():
    key_row = np.full((1, 256), -100, np.int32)
    key_col = np.full((1, 256), -100, np.int32)

    def put(slot, r, c):
        key_row[0, slot] = r
        key_col[0, slot] = c

    for r in range(7):
        for c in range(7):
            put(8 * r + c, r, c)
    for s in range(3):
        for c in range(7):
            put(SLOTS["up"] + 8 * s + c, s - 3, c)
            put(SLOTS["dn"] + 8 * s + c, 7 + s, c)
            put(SLOTS["lf"] + 8 * s + c, c, s - 3)
            put(SLOTS["rt"] + 8 * s + c, c, 7 + s)
        for u in range(3):
            put(SLOTS["ul"] + 3 * s + u, s - 3, u - 3)
            put(SLOTS["ur"] + 3 * s + u, s - 3, 7 + u)
            put(SLOTS["dl"] + 3 * s + u, 7 + s, u - 3)
            put(SLOTS["dr"] + 3 * s + u, 7 + s, 7 + u)
    perm = np.zeros((256, 256), np.float32)
    for slot in range(256):
        if key_row[0, slot] > -100:
            perm[(key_row[0, slot] + 3) * 16 + key_col[0, slot] + 3, slot] = 1
    pick = np.zeros((128, 64), np.float32)
    for s in range(3):
        for r in range(7):
            pick[8 * s + r, 8 * r + s] = 1
            pick[32 + 8 * s + r, 8 * r + 4 + s] = 1
        for u in range(3):
            pick[64 + 3 * s + u, 8 * s + u] = 1
            pick[80 + 3 * s + u, 8 * s + 4 + u] = 1
            pick[96 + 3 * s + u, 8 * (4 + s) + u] = 1
            pick[112 + 3 * s + u, 8 * (4 + s) + 4 + u] = 1
    return key_row, key_col, perm, pick


KEY_ROW, KEY_COL, PERM, PICK = tables()


def nn(a, b):
    return lax.dot_general(a, b, (((1,), (0,)), ((), ())), preferred_element_type=F32)


def nt(a, b):
    return lax.dot_general(a, b, (((1,), (1,)), ((), ())), preferred_element_type=F32)


def tn(a, b):
    return lax.dot_general(a, b, (((0,), (0,)), ((), ())), preferred_element_type=F32)


def three_parts(x):
    high = x.astype(BF)
    rest = x - high.astype(F32)
    mid = rest.astype(BF)
    low = (rest - mid.astype(F32)).astype(BF)
    return high, mid, low


def front_kernel(s_ref, x_ref, og_ref, gain_ref, wqkv_ref, wproj_ref, pick_ref, q_ref, kv_ref, ag_ref, m1_ref, nb_ref, ogk_ref, nx_ref, inv_ref, up_ref, dn_ref, lf_ref, rt_ref, ul_ref, ur_ref, dl_ref, dr_ref, xs, os):
    xs[...] = jnp.zeros_like(xs)
    os[...] = jnp.zeros_like(os)
    for t in range(3):
        for r in range(7):
            xs[t * 64 + r * 8 : t * 64 + r * 8 + 7, :] = x_ref[t, r].astype(F32)
            os[t * 64 + r * 8 : t * 64 + r * 8 + 7, :] = og_ref[t, r].astype(F32)
    xf = xs[...]
    dev = xf - jnp.mean(xf, axis=-1, keepdims=True)
    inv = lax.rsqrt(jnp.mean(dev * dev, axis=-1, keepdims=True) + EPS)
    nx = dev * inv
    nx_ref[...] = nx
    inv_ref[...] = jnp.broadcast_to(inv, inv_ref.shape)
    normed = (nx * gain_ref[...]).astype(BF)
    nb_ref[...] = normed
    qkv = nn(normed, wqkv_ref[...]).astype(BF)
    for t in range(3):
        rows = qkv[t * 64 : t * 64 + 64]
        q_ref[t] = rows[:, :512]
        kv = rows[:, 512:]
        kv_ref[t] = kv
        up_ref[t] = kv[0:24]
        dn_ref[t] = kv[32:56]
        out = nn(pick_ref[...], kv).astype(BF)
        lf_ref[t] = out[0:24]
        rt_ref[t] = out[32:56]
        ul_ref[t] = out[64:80]
        ur_ref[t] = out[80:96]
        dl_ref[t] = out[96:112]
        dr_ref[t] = out[112:128]
    og = os[...].astype(BF)
    ag_ref[...] = nt(og, wproj_ref[...]).astype(BF).reshape(3, 64, 512)
    m1_ref[:, :1024] = normed

    @pl.when(s_ref[0] == 0)
    def _():
        ogk_ref[...] = og[:, :512]
        m1_ref[:, 1024:] = og[:, 512:]

    @pl.when(s_ref[0] != 0)
    def _():
        ogk_ref[...] = og[:, 512:]
        m1_ref[:, 1024:] = og[:, :512]


def table_kernel(s_ref, rel_ref, key_row_ref, key_col_ref, perm_ref, out_ref, grid_ref):
    grid_ref[...] = jnp.zeros_like(grid_ref)
    line = rel_ref[...]
    for r in range(7):
        for c in range(7):
            turned = pltpu.roll(line, ((r - 3) * 16 + c - 3) % 256, 1)
            for half in range(2):
                grid_ref[half, pl.ds(r * 8 + c, 8, stride=64), :] = turned[:, half * 128 : half * 128 + 128]
    high, mid, low = three_parts(jnp.concatenate([grid_ref[0], grid_ref[1]], axis=1))
    perm = perm_ref[...]
    table = nn(high, perm) + (nn(mid, perm) + nn(low, perm))
    place = lax.broadcasted_iota(jnp.int32, (64, 256), 0)
    row = place // 8
    col = place % 8
    row_first = jnp.clip(s_ref[1] + row - 3, 0, s_ref[3] - WIN) - s_ref[1]
    col_first = jnp.clip(s_ref[2] + col - 3, 0, s_ref[4] - WIN) - s_ref[2]
    key_row = key_row_ref[...]
    key_col = key_col_ref[...]
    valid = (key_row >= row_first) & (key_row < row_first + WIN) & (key_col >= col_first) & (key_col < col_first + WIN) & (row < 7) & (col < 7)
    for h in range(8):
        out_ref[h * 64 : h * 64 + 64, :] = jnp.where(valid, table[h * 64 : h * 64 + 64], -1e30)


def attention_kernel(q_ref, kv_ref, ag_ref, table_ref, *refs):
    got = dict(zip(PIECES, refs[:8]))
    att_ref, dq_ref, own_ref, g_ref = refs[8:12]
    back = dict(zip(PIECES, refs[12:20]))
    keys, dkv = refs[20:]
    keys[...] = jnp.zeros_like(keys)
    at_row = lax.broadcasted_iota(jnp.int32, (256, 256), 0) // 64
    at_col = lax.broadcasted_iota(jnp.int32, (256, 256), 1) // 64
    diag = at_row == at_col

    def spread(x):
        x = x.astype(F32)
        return jnp.where(diag, jnp.concatenate([x, x, x, x], axis=0), 0.0).astype(BF)

    def gather(x):
        x = jnp.where(diag, x, 0.0)
        return (x[0:64] + x[64:128]) + (x[128:192] + x[192:256])

    totals = [None, None]
    for t in range(3):
        keys[t, 0:64] = kv_ref[t]
        for name in PIECES:
            keys[t, SLOTS[name] : SLOTS[name] + ROWS[name]] = got[name][t]
        for g in range(2):
            at = slice(g * 256, g * 256 + 256)
            k = keys[t, :, g * 256 : g * 256 + 256]
            v = keys[t, :, 512 + g * 256 : 768 + g * 256]
            qb = spread(q_ref[t, :, at])
            db = spread(ag_ref[t, :, at])
            scores = nt(qb, k) * 0.125 + table_ref[at, :]
            terms = jnp.exp(scores - jnp.max(scores, axis=-1, keepdims=True))
            probs = terms / jnp.sum(terms, axis=-1, keepdims=True)
            low = probs.astype(BF)
            att_ref[t, :, at] = gather(nn(low, v)).astype(BF)
            dprobs = nt(db, v)
            dscores = probs * (dprobs - jnp.sum(probs * dprobs, axis=-1, keepdims=True))
            totals[g] = dscores if t == 0 else totals[g] + dscores
            dlow = dscores.astype(BF)
            dq_ref[t, :, at] = (gather(nn(dlow, k)) * 0.125).astype(BF)
            dkv[:, g * 256 : g * 256 + 256] = tn(dlow, qb) * 0.125
            dkv[:, 512 + g * 256 : 768 + g * 256] = tn(low, db)
        own_ref[t] = dkv[0:64]
        for name in PIECES:
            back[name][t] = dkv[SLOTS[name] : SLOTS[name] + ROWS[name], :].astype(BF)
    g_ref[0:256] = totals[0]
    g_ref[256:512] = totals[1]


def out_kernel(att_ref, wproj_ref, x_ref, g_ref, perm_ref, out_ref, bias_ref, ys, gs):
    ys[...] = nn(att_ref[...].reshape(192, 512), wproj_ref[...])
    for t in range(3):
        for r in range(7):
            out_ref[t, r] = (x_ref[t, r].astype(F32) + ys[t * 64 + r * 8 : t * 64 + r * 8 + 7, :]).astype(BF)
    high, mid, low = three_parts(g_ref[...])
    perm = perm_ref[...]
    grid = nt(high, perm) + (nt(mid, perm) + nt(low, perm))
    for half in range(2):
        gs[half] = grid[:, half * 128 : half * 128 + 128]
    total = None
    for r in range(7):
        for c in range(7):
            part = jnp.concatenate([gs[half, pl.ds(r * 8 + c, 8, stride=64), :] for half in range(2)], axis=1)
            part = pltpu.roll(part, ((3 - r) * 16 + 3 - c) % 256, 1)
            total = part if total is None else total + part
    bias_ref[...] = total


def join_kernel(s_ref, own_ref, dq_ref, att_ref, pick_ref, up_ref, dn_ref, lf_ref, rt_ref, ul_ref, ur_ref, dl_ref, dr_ref, dqkv_ref, m2_ref, side, acc):
    side[...] = jnp.zeros_like(side)
    for t in range(3):
        side[t, 0:24] = lf_ref[t]
        side[t, 32:56] = rt_ref[t]
        side[t, 64:80] = ul_ref[t]
        side[t, 80:96] = ur_ref[t]
        side[t, 96:112] = dl_ref[t]
        side[t, 112:128] = dr_ref[t]
        acc[...] = own_ref[t] + tn(pick_ref[...], side[t])
        acc[0:24] = acc[0:24] + up_ref[t].astype(F32)
        acc[32:56] = acc[32:56] + dn_ref[t].astype(F32)
        dqkv_ref[t * 64 : t * 64 + 64, 0:512] = dq_ref[t]
        dqkv_ref[t * 64 : t * 64 + 64, 512:1536] = acc[...].astype(BF)
    m2_ref[:, 0:512] = att_ref[...].reshape(192, 512)

    @pl.when(s_ref[0] == 0)
    def _():
        m2_ref[:, 512:1280] = dqkv_ref[:, 768:1536]

    @pl.when(s_ref[0] != 0)
    def _():
        m2_ref[:, 512:1280] = dqkv_ref[:, 0:768]


def feats_kernel(dqkv_ref, wqkv_ref, nx_ref, inv_ref, gain_ref, og_ref, out_ref, gg_ref, ys):
    ngrad = nt(dqkv_ref[...], wqkv_ref[...])
    nx = nx_ref[...]
    gg_ref[...] = jnp.sum(ngrad * nx, axis=0, keepdims=True)
    scaled = ngrad * gain_ref[...]
    correction = scaled - jnp.mean(scaled, axis=-1, keepdims=True) - nx * jnp.mean(scaled * nx, axis=-1, keepdims=True)
    ys[...] = inv_ref[:, 0:1] * correction
    for t in range(3):
        for r in range(7):
            out_ref[t, r] = (og_ref[t, r].astype(F32) + ys[t * 64 + r * 8 : t * 64 + r * 8 + 7, :]).astype(BF)


def put_small(write, bias, gain_rows):
    high = bias.astype(BF)
    write(slice(0, 256), high)
    write(slice(256, 512), (bias - high.astype(F32)).astype(BF))
    high = gain_rows.astype(BF)
    write(slice(512, 640), high)
    write(slice(640, 768), (gain_rows - high.astype(F32)).astype(BF))
    write(slice(768, 1024), jnp.zeros((8, 256), BF))


def get_small(block):
    return block[:, 0:256] + block[:, 256:512], block[:, 512:640] + block[:, 640:768]


def weights_kernel(s_ref, nb_ref, att_ref, dqkv_ref, ogk_ref, m1_ref, m2_ref, gg_ref, bias_ref, out_ref, zq, zp, gs):
    count = out_ref.shape[0]
    tall = 1024 // count

    @pl.when(s_ref[0] == 0)
    def _():
        zq[...] = tn(nb_ref[...], dqkv_ref[:, 0:768]) + tn(m1_ref[:, 0:1024], m2_ref[:, 512:1280])

    @pl.when(s_ref[0] != 0)
    def _():
        zq[...] = tn(nb_ref[...], dqkv_ref[:, 768:1536]) + tn(m1_ref[:, 0:1024], m2_ref[:, 512:1280])

    zp[...] = tn(att_ref[...].reshape(192, 512), ogk_ref[...]) + tn(m2_ref[:, 0:512], m1_ref[:, 1024:1536])
    for j in range(8):
        gs[j : j + 1, :] = gg_ref[:, j * 128 : j * 128 + 128]
    for i in range(count):
        out_ref[i, 0:tall, 0:768] = zq[i * tall : i * tall + tall].astype(BF)
        first = i * tall
        out_ref[i, 0:tall, 768:1024] = zp[first % 512 : first % 512 + tall, first // 512 * 256 : first // 512 * 256 + 256].astype(BF)

        def write(lanes, value, i=i):
            out_ref[i, tall : tall + 8, lanes] = value

        put_small(write, bias_ref[...], gs[...])


def first_sum_kernel(y_ref, out_ref):
    count = y_ref.shape[0]
    total = y_ref[0].astype(F32)
    for i in range(1, count):
        total = total + y_ref[i].astype(F32)
    groups = out_ref.shape[0]
    tall = out_ref.shape[1] - 8
    bias, gain_rows = get_small(total[groups * tall : groups * tall + 8])
    for j in range(groups):
        out_ref[j, 0:tall] = total[j * tall : j * tall + tall].astype(BF)

        def write(lanes, value, j=j):
            out_ref[j, tall : tall + 8, lanes] = value

        put_small(write, bias, gain_rows)


def second_sum_kernel(y_ref, out_ref, small_ref):
    count = y_ref.shape[0]
    total = y_ref[0].astype(F32)
    for i in range(1, count):
        total = total + y_ref[i].astype(F32)
    tall = out_ref.shape[1]
    shard = total[0:tall].astype(BF)
    for j in range(out_ref.shape[0]):
        out_ref[j] = shard
    bias, gain_rows = get_small(total[tall : tall + 8])

    def write(lanes, value):
        small_ref[:, lanes] = value

    put_small(write, bias, gain_rows)


def last_kernel(s_ref, mine_ref, theirs_ref, small_ref, other_ref, qkv_ref, proj_ref, gain_ref, bias_ref):
    @pl.when(s_ref[0] == 0)
    def _():
        for c, ref in ((0, mine_ref), (1, theirs_ref)):
            qkv_ref[:, c * 768 : c * 768 + 768] = ref[:, 0:768]
            for j in range(2):
                proj_ref[:, c * 512 + j * 256 : c * 512 + j * 256 + 256] = ref[j * 512 : j * 512 + 512, 768:1024]

    @pl.when(s_ref[0] != 0)
    def _():
        for c, ref in ((1, mine_ref), (0, theirs_ref)):
            qkv_ref[:, c * 768 : c * 768 + 768] = ref[:, 0:768]
            for j in range(2):
                proj_ref[:, c * 512 + j * 256 : c * 512 + j * 256 + 256] = ref[j * 512 : j * 512 + 512, 768:1024]

    bias0, gain0 = get_small(small_ref[...].astype(F32))
    bias1, gain1 = get_small(other_ref[...].astype(F32))
    gain_ref[...] = gain0 + gain1
    bias_ref[...] = bias0 + bias1


def call(kernel, outs, args, scratch=(), name=None):
    specs = [pl.BlockSpec(memory_space=pltpu.SMEM) if a.dtype == jnp.int32 and a.ndim == 1 else pl.BlockSpec(memory_space=pltpu.VMEM) for a in args]
    return pl.pallas_call(
        kernel,
        out_shape=[jax.ShapeDtypeStruct(shape, kind) for shape, kind in outs],
        in_specs=specs,
        out_specs=[pl.BlockSpec(memory_space=pltpu.VMEM) for _ in outs],
        scratch_shapes=[pltpu.VMEM(shape, kind) for shape, kind in scratch],
        compiler_params=pltpu.CompilerParams(vmem_limit_bytes=48 * 1024 * 1024),
        interpret=INTERPRET,
        name=name,
    )(*args)


def make_body(sizes):
    zl, nx_, zh, ny, nc = sizes
    rows, cols = zl * nx_, zh * ny * nc
    every = ("zl", "x", "zh", "y", "c")
    row_axes = ("zl", "x")
    col_axes = ("zh", "y")
    groups = zh * ny

    def move(value, row_step, col_step):
        pairs = []
        for i in range(rows):
            for j in range(cols):
                if 0 <= i + row_step < rows and 0 <= j + col_step < cols:
                    pairs.append((i * cols + j, (i + row_step) * cols + j + col_step))
        return lax.ppermute(value, every, pairs)

    def swap(value):
        return lax.ppermute(value, "c", [(0, 1), (1, 0)])

    def body(image_feats, norm_gain, w_qkv, rel_bias, w_proj, out_grad):
        core = lax.axis_index("c")
        row_anchor = (lax.axis_index("zl") * nx_ + lax.axis_index("x")) * 7
        col_anchor = ((lax.axis_index("zh") * ny + lax.axis_index("y")) * nc + core) * 7
        scalars = jnp.stack([core, row_anchor, col_anchor, jnp.int32(rows * 7), jnp.int32(cols * 7)]).astype(jnp.int32)
        gain = norm_gain.reshape(1, 1024)
        pick = jnp.asarray(PICK, BF)
        perm = jnp.asarray(PERM, BF)
        rel = jnp.pad(rel_bias, ((0, 0), (0, 3), (0, 3))).reshape(8, 256)
        front = call(
            front_kernel,
            [((3, 64, 512), BF), ((3, 64, 1024), BF), ((3, 64, 512), BF), ((192, 1536), BF), ((192, 1024), BF), ((192, 512), BF), ((192, 1024), F32), ((192, 128), F32)]
            + [((3, ROWS[name], 1024), BF) for name in PIECES],
            [scalars, image_feats, out_grad, gain, w_qkv, w_proj, pick],
            [((192, 1024), F32), ((192, 1024), F32)],
            "front",
        )
        queries, own_kv, attn_grad, m1, normed, og_keep, normal_x, inv_std = front[:8]
        facing = {"up": "dn", "dn": "up", "lf": "rt", "rt": "lf", "ul": "dr", "ur": "dl", "dl": "ur", "dr": "ul"}
        leaving = dict(zip(PIECES, front[8:]))
        got = {facing[name]: move(leaving[name], *COMES[name]) for name in PIECES}
        m1_other = swap(m1)
        (table,) = call(
            table_kernel,
            [((512, 256), F32)],
            [scalars, rel, jnp.asarray(KEY_ROW), jnp.asarray(KEY_COL), perm],
            [((2, 512, 128), F32)],
            "table",
        )
        mid = call(
            attention_kernel,
            [((3, 64, 512), BF), ((3, 64, 512), BF), ((3, 64, 1024), F32), ((512, 256), F32)] + [((3, ROWS[name], 1024), BF) for name in PIECES],
            [queries, own_kv, attn_grad, table] + [got[name] for name in PIECES],
            [((3, 256, 1024), BF), ((256, 1024), F32)],
            "attention",
        )
        attended, query_grad, own_grad, score_sum = mid[:4]
        back = dict(zip(PIECES, mid[4:]))
        home = {facing[name]: move(back[name], *COMES[name]) for name in PIECES}
        layer_out, bias_part = call(
            out_kernel,
            [((3, 7, 7, 1024), BF), ((8, 256), F32)],
            [attended, w_proj, image_feats, score_sum, perm],
            [((192, 1024), F32), ((2, 512, 128), F32)],
            "layer_out",
        )
        dqkv, m2 = call(
            join_kernel,
            [((192, 1536), BF), ((192, 1280), BF)],
            [scalars, own_grad, query_grad, attended, pick] + [home[name] for name in PIECES],
            [((3, 128, 1024), BF), ((64, 1024), F32)],
            "join",
        )
        m2_other = swap(m2)
        feats_grad, gain_part = call(
            feats_kernel,
            [((3, 7, 7, 1024), BF), ((1, 1024), F32)],
            [dqkv, w_qkv, normal_x, inv_std, gain, out_grad],
            [((192, 1024), F32)],
            "feats",
        )
        tall1 = 1024 // rows
        tall2 = tall1 // groups
        (send,) = call(
            weights_kernel,
            [((rows, tall1 + 8, 1024), BF)],
            [scalars, normed, attended, dqkv, og_keep, m1_other, m2_other, gain_part, bias_part],
            [((1024, 768), F32), ((512, 512), F32), ((8, 128), F32)],
            "weights",
        )
        send = lax.all_to_all(send, row_axes, 0, 0, tiled=True)
        (send,) = call(first_sum_kernel, [((groups, tall2 + 8, 1024), BF)], [send], (), "first_sum")
        send = lax.all_to_all(send, col_axes, 0, 0, tiled=True)
        send, small = call(second_sum_kernel, [((groups, tall2, 1024), BF), ((8, 1024), BF)], [send], (), "second_sum")
        small_other = swap(small)
        part = lax.all_to_all(send, col_axes, 0, 0, tiled=True).reshape(1, tall1, 1024)
        part = lax.all_to_all(jnp.broadcast_to(part, (rows, tall1, 1024)), row_axes, 0, 0, tiled=True)
        mine = part.reshape(1024, 1024)
        theirs = swap(mine)
        qkv_grad, proj_grad, gain_grad, bias_grad = call(
            last_kernel,
            [((1024, 1536), BF), ((512, 1024), BF), ((8, 128), F32), ((8, 256), F32)],
            [scalars, mine, theirs, small, small_other],
            (),
            "last",
        )
        return (layer_out, feats_grad, qkv_grad, proj_grad, gain_grad.reshape(1024), bias_grad.reshape(8, 16, 16)[:, :13, :13])

    return body


def solution(mesh, sizes=(2, 4, 4, 4, 2)):
    fine = Mesh(mesh.devices.reshape(sizes), ("zl", "x", "zh", "y", "c"))
    image = P(None, ("zl", "x"), ("zh", "y", "c"), None)
    return jax.shard_map(
        make_body(sizes),
        mesh=fine,
        in_specs=(image, P(), P(), P(), P(), image),
        out_specs=(image, image, P(), P(), P(), P()),
        check_vma=False,
    )
```

```python
import numpy as np
import jax
import jax.numpy as jnp
from jax import lax
from jax.experimental import pallas as pl
from jax.experimental.pallas import tpu as pltpu
from jax.sharding import Mesh
from jax.sharding import PartitionSpec as P

WIN = 7
EPS = 1e-05
BF = jnp.bfloat16
F32 = jnp.float32
INTERPRET = False

UP, DN, LF, RT = 64, 96, 128, 176


def tables():
    key_row = np.full((1, 256), -100, np.int32)
    key_col = np.full((1, 256), -100, np.int32)
    for r in range(7):
        for c in range(7):
            key_row[0, 8 * r + c] = r
            key_col[0, 8 * r + c] = c
    for s in range(3):
        for c in range(7):
            for slot, row in ((UP, s - 3), (DN, 7 + s)):
                key_row[0, slot + 8 * s + c] = row
                key_col[0, slot + 8 * s + c] = c
        for r in range(13):
            for slot, col in ((LF, s - 3), (RT, 7 + s)):
                key_row[0, slot + 16 * s + r] = r - 3
                key_col[0, slot + 16 * s + r] = col
    perm = np.zeros((256, 256), np.float32)
    for slot in range(256):
        if key_row[0, slot] > -100:
            perm[(key_row[0, slot] + 3) * 16 + key_col[0, slot] + 3, slot] = 1
    pick = np.zeros((96, 128), np.float32)
    for s in range(3):
        for r in range(13):
            row = r - 3
            start = UP + 8 * r if row < 0 else (DN + 8 * (row - 7) if row > 6 else 8 * row)
            pick[16 * s + r, start + s] = 1
            pick[48 + 16 * s + r, start + 4 + s] = 1
    return key_row, key_col, perm, pick


KEY_ROW, KEY_COL, PERM, PICK = tables()


def nn(a, b):
    return lax.dot_general(a, b, (((1,), (0,)), ((), ())), preferred_element_type=F32)


def nt(a, b):
    return lax.dot_general(a, b, (((1,), (1,)), ((), ())), preferred_element_type=F32)


def tn(a, b):
    return lax.dot_general(a, b, (((0,), (0,)), ((), ())), preferred_element_type=F32)


def three_parts(x):
    high = x.astype(BF)
    rest = x - high.astype(F32)
    mid = rest.astype(BF)
    low = (rest - mid.astype(F32)).astype(BF)
    return high, mid, low


def front_kernel(s_ref, x_hbm, og_hbm, gain_ref, wqkv_hbm, wproj_hbm, q_ref, kv_ref, ag_ref, m1_ref, nb_ref, ogk_ref, nx_ref, inv_ref, a_ref, b_ref, xs, os, x_ref, og_ref, wqkv_ref, wproj_ref, sems):
    loads = [
        pltpu.make_async_copy(source, target, sems.at[i])
        for i, (source, target) in enumerate(((x_hbm, x_ref), (og_hbm, og_ref), (wqkv_hbm, wqkv_ref), (wproj_hbm, wproj_ref)))
    ]
    for load in loads:
        load.start()
    xs[...] = jnp.zeros_like(xs)
    os[...] = jnp.zeros_like(os)
    loads[0].wait()
    for t in range(3):
        for r in range(7):
            xs[t * 64 + r * 8 : t * 64 + r * 8 + 7, :] = x_ref[t, r].astype(F32)
    xf = xs[...]
    dev = xf - jnp.mean(xf, axis=-1, keepdims=True)
    inv = lax.rsqrt(jnp.mean(dev * dev, axis=-1, keepdims=True) + EPS)
    nx = dev * inv
    nx_ref[...] = nx
    inv_ref[...] = jnp.broadcast_to(inv, inv_ref.shape)
    normed = (nx * gain_ref[...]).astype(BF)
    nb_ref[...] = normed
    m1_ref[:, :1024] = normed
    loads[2].wait()
    qkv = nn(normed, wqkv_ref[...]).astype(BF)
    for t in range(3):
        rows = qkv[t * 64 : t * 64 + 64]
        q_ref[t] = rows[:, :512]
        kv_ref[t] = rows[:, 512:]

    @pl.when(s_ref[5] == 0)
    def _():
        for t in range(3):
            a_ref[t] = kv_ref[t, 32:56]
            b_ref[t] = kv_ref[t, 0:24]

    @pl.when(s_ref[5] != 0)
    def _():
        for t in range(3):
            a_ref[t] = kv_ref[t, 0:24]
            b_ref[t] = kv_ref[t, 32:56]

    loads[1].wait()
    for t in range(3):
        for r in range(7):
            os[t * 64 + r * 8 : t * 64 + r * 8 + 7, :] = og_ref[t, r].astype(F32)
    og = os[...].astype(BF)
    loads[3].wait()
    ag_ref[...] = nt(og, wproj_ref[...]).astype(BF).reshape(3, 64, 512)

    @pl.when(s_ref[0] == 0)
    def _():
        ogk_ref[...] = og[:, :512]
        m1_ref[:, 1024:] = og[:, 512:]

    @pl.when(s_ref[0] != 0)
    def _():
        ogk_ref[...] = og[:, 512:]
        m1_ref[:, 1024:] = og[:, :512]


def columns_kernel(s_ref, kv_ref, got_a, got_b, pick_ref, edge_ref, a_ref, b_ref, rows):
    edge_ref[...] = jnp.zeros_like(edge_ref)

    @pl.when(s_ref[5] == 0)
    def _():
        for t in range(3):
            edge_ref[t, 0:24] = got_b[t]
            edge_ref[t, 32:56] = got_a[t]

    @pl.when(s_ref[5] != 0)
    def _():
        for t in range(3):
            edge_ref[t, 0:24] = got_a[t]
            edge_ref[t, 32:56] = got_b[t]

    for t in range(3):
        rows[t, 0:64] = kv_ref[t]
        rows[t, 64:128] = edge_ref[t]
    outs = [nn(pick_ref[...], rows[t]).astype(BF) for t in range(3)]

    @pl.when(s_ref[0] == 0)
    def _():
        for t in range(3):
            a_ref[t] = outs[t][48:96]
            b_ref[t] = outs[t][0:48]

    @pl.when(s_ref[0] != 0)
    def _():
        for t in range(3):
            a_ref[t] = outs[t][0:48]
            b_ref[t] = outs[t][48:96]


def table_kernel(s_ref, rel_ref, key_row_ref, key_col_ref, perm_ref, out_ref, grid_ref):
    grid_ref[...] = jnp.zeros_like(grid_ref)
    line = rel_ref[...]
    for r in range(7):
        for c in range(7):
            turned = pltpu.roll(line, ((r - 3) * 16 + c - 3) % 256, 1)
            for half in range(2):
                grid_ref.at[half][pl.ds(r * 8 + c, 8, stride=64), :] = turned[:, half * 128 : half * 128 + 128]
    high, mid, low = three_parts(jnp.concatenate([grid_ref[0], grid_ref[1]], axis=1))
    perm = perm_ref[...]
    table = nn(high, perm) + (nn(mid, perm) + nn(low, perm))
    place = lax.broadcasted_iota(jnp.int32, (64, 256), 0)
    row = place // 8
    col = place % 8
    row_first = jnp.clip(s_ref[1] + row - 3, 0, s_ref[3] - WIN) - s_ref[1]
    col_first = jnp.clip(s_ref[2] + col - 3, 0, s_ref[4] - WIN) - s_ref[2]
    key_row = key_row_ref[...]
    key_col = key_col_ref[...]
    valid = (key_row >= row_first) & (key_row < row_first + WIN) & (key_col >= col_first) & (key_col < col_first + WIN) & (row < 7) & (col < 7)
    for h in range(8):
        out_ref[h * 64 : h * 64 + 64, :] = jnp.where(valid, table[h * 64 : h * 64 + 64], -1e30)


def attention_kernel(s_ref, q_ref, kv_ref, edge_ref, got_a, got_b, ag_ref, table_ref, att_ref, dq_ref, own_ref, a_ref, b_ref, g_ref, keys, dkv):
    keys[:, 224:256, :] = jnp.zeros((3, 32, 1024), BF)
    for t in range(3):
        keys[t, 0:64] = kv_ref[t]
        keys[t, 64:128] = edge_ref[t]

    @pl.when(s_ref[0] == 0)
    def _():
        for t in range(3):
            keys[t, LF : LF + 48] = got_b[t]
            keys[t, RT : RT + 48] = got_a[t]

    @pl.when(s_ref[0] != 0)
    def _():
        for t in range(3):
            keys[t, LF : LF + 48] = got_a[t]
            keys[t, RT : RT + 48] = got_b[t]

    at_row = lax.broadcasted_iota(jnp.int32, (256, 256), 0) // 64
    at_col = lax.broadcasted_iota(jnp.int32, (256, 256), 1) // 64
    diag = at_row == at_col

    def spread(x):
        x = x.astype(F32)
        return jnp.where(diag, jnp.concatenate([x, x, x, x], axis=0), 0.0).astype(BF)

    def gather(x):
        x = jnp.where(diag, x, 0.0)
        return (x[0:64] + x[64:128]) + (x[128:192] + x[192:256])

    totals = [None, None]
    for t in range(3):
        for g in range(2):
            at = slice(g * 256, g * 256 + 256)
            k = keys[t, :, g * 256 : g * 256 + 256]
            v = keys[t, :, 512 + g * 256 : 768 + g * 256]
            qb = spread(q_ref[t, :, at])
            db = spread(ag_ref[t, :, at])
            scores = nt(qb, k) * 0.125 + table_ref[at, :]
            terms = jnp.exp(scores - jnp.max(scores, axis=-1, keepdims=True))
            probs = terms / jnp.sum(terms, axis=-1, keepdims=True)
            low = probs.astype(BF)
            att_ref[t, :, at] = gather(nn(low, v)).astype(BF)
            dprobs = nt(db, v)
            dscores = probs * (dprobs - jnp.sum(probs * dprobs, axis=-1, keepdims=True))
            totals[g] = dscores if t == 0 else totals[g] + dscores
            dlow = dscores.astype(BF)
            dq_ref[t, :, at] = (gather(nn(dlow, k)) * 0.125).astype(BF)
            for lanes, grad in ((at, tn(dlow, qb) * 0.125), (slice(512 + g * 256, 768 + g * 256), tn(low, db))):
                own_ref[t, :, lanes] = grad[0:128]
                dkv[t, :, lanes] = grad[128:224].astype(BF)

    @pl.when(s_ref[0] == 0)
    def _():
        for t in range(3):
            a_ref[t] = dkv[t, 48:96]
            b_ref[t] = dkv[t, 0:48]

    @pl.when(s_ref[0] != 0)
    def _():
        for t in range(3):
            a_ref[t] = dkv[t, 0:48]
            b_ref[t] = dkv[t, 48:96]

    g_ref[0:256] = totals[0]
    g_ref[256:512] = totals[1]


def out_kernel(att_ref, wproj_ref, x_ref, g_ref, perm_ref, out_ref, bias_ref, ys, gs):
    ys[...] = nn(att_ref[...].reshape(192, 512), wproj_ref[...])
    for t in range(3):
        for r in range(7):
            out_ref[t, r] = (x_ref[t, r].astype(F32) + ys[t * 64 + r * 8 : t * 64 + r * 8 + 7, :]).astype(BF)
    high, mid, low = three_parts(g_ref[...])
    perm = perm_ref[...]
    grid = nt(high, perm) + (nt(mid, perm) + nt(low, perm))
    for half in range(2):
        gs[half] = grid[:, half * 128 : half * 128 + 128]
    total = None
    for r in range(7):
        for c in range(7):
            part = jnp.concatenate([gs.at[half][pl.ds(r * 8 + c, 8, stride=64), :] for half in range(2)], axis=1)
            part = pltpu.roll(part, ((3 - r) * 16 + 3 - c) % 256, 1)
            total = part if total is None else total + part
    bias_ref[...] = total


def edges_kernel(s_ref, own_ref, pick_ref, got_a, got_b, sum_ref, a_ref, b_ref, side):
    @pl.when(s_ref[0] == 0)
    def _():
        for t in range(3):
            side[t, 0:48] = got_b[t]
            side[t, 48:96] = got_a[t]

    @pl.when(s_ref[0] != 0)
    def _():
        for t in range(3):
            side[t, 0:48] = got_a[t]
            side[t, 48:96] = got_b[t]

    totals = [own_ref[t] + tn(pick_ref[...], side[t]) for t in range(3)]
    for t in range(3):
        sum_ref[t] = totals[t][0:64]

    @pl.when(s_ref[5] == 0)
    def _():
        for t in range(3):
            a_ref[t] = totals[t][96:120].astype(BF)
            b_ref[t] = totals[t][64:88].astype(BF)

    @pl.when(s_ref[5] != 0)
    def _():
        for t in range(3):
            a_ref[t] = totals[t][64:88].astype(BF)
            b_ref[t] = totals[t][96:120].astype(BF)


def join_kernel(s_ref, sum_ref, dq_ref, att_ref, got_a, got_b, bias_ref, dqkv_ref, m2_ref, acc):
    acc[...] = sum_ref[...]

    @pl.when(s_ref[5] == 0)
    def _():
        for t in range(3):
            acc[t, 32:56] = acc[t, 32:56] + got_a[t].astype(F32)
            acc[t, 0:24] = acc[t, 0:24] + got_b[t].astype(F32)

    @pl.when(s_ref[5] != 0)
    def _():
        for t in range(3):
            acc[t, 0:24] = acc[t, 0:24] + got_a[t].astype(F32)
            acc[t, 32:56] = acc[t, 32:56] + got_b[t].astype(F32)

    for t in range(3):
        dqkv_ref[t * 64 : t * 64 + 64, 0:512] = dq_ref[t]
        dqkv_ref[t * 64 : t * 64 + 64, 512:1536] = acc[t].astype(BF)
    m2_ref[:, 0:512] = att_ref[...].reshape(192, 512)

    @pl.when(s_ref[0] == 0)
    def _():
        m2_ref[:, 512:1280] = dqkv_ref[:, 768:1536]

    @pl.when(s_ref[0] != 0)
    def _():
        m2_ref[:, 512:1280] = dqkv_ref[:, 0:768]


def feats_kernel(dqkv_ref, wqkv_ref, nx_ref, inv_ref, gain_ref, og_ref, out_ref, gg_ref, ys):
    ngrad = nt(dqkv_ref[...], wqkv_ref[...])
    nx = nx_ref[...]
    gg_ref[...] = jnp.sum(ngrad * nx, axis=0, keepdims=True)
    scaled = ngrad * gain_ref[...]
    correction = scaled - jnp.mean(scaled, axis=-1, keepdims=True) - nx * jnp.mean(scaled * nx, axis=-1, keepdims=True)
    ys[...] = inv_ref[:, 0:1] * correction
    for t in range(3):
        for r in range(7):
            out_ref[t, r] = (og_ref[t, r].astype(F32) + ys[t * 64 + r * 8 : t * 64 + r * 8 + 7, :]).astype(BF)


def put_small(write, bias, gain_rows):
    high = bias.astype(BF)
    write(slice(0, 256), high)
    write(slice(256, 512), (bias - high.astype(F32)).astype(BF))
    high = gain_rows.astype(BF)
    write(slice(512, 640), high)
    write(slice(640, 768), (gain_rows - high.astype(F32)).astype(BF))
    write(slice(768, 1024), jnp.zeros((8, 256), BF))


def get_small(block):
    return block[:, 0:256] + block[:, 256:512], block[:, 512:640] + block[:, 640:768]


def weights_kernel(s_ref, nb_ref, att_ref, dqkv_ref, ogk_ref, m1_ref, m2_ref, gg_ref, bias_ref, out_ref, zq, zp, gs):
    count = out_ref.shape[0]
    tall = 1024 // count

    @pl.when(s_ref[0] == 0)
    def _():
        zq[...] = tn(nb_ref[...], dqkv_ref[:, 0:768]) + tn(m1_ref[:, 0:1024], m2_ref[:, 512:1280])

    @pl.when(s_ref[0] != 0)
    def _():
        zq[...] = tn(nb_ref[...], dqkv_ref[:, 768:1536]) + tn(m1_ref[:, 0:1024], m2_ref[:, 512:1280])

    zp[...] = tn(att_ref[...].reshape(192, 512), ogk_ref[...]) + tn(m2_ref[:, 0:512], m1_ref[:, 1024:1536])
    for j in range(8):
        gs[j : j + 1, :] = gg_ref[:, j * 128 : j * 128 + 128]
    for i in range(count):
        out_ref[i, 0:tall, 0:768] = zq[i * tall : i * tall + tall].astype(BF)
        first = i * tall
        out_ref[i, 0:tall, 768:1024] = zp[first % 512 : first % 512 + tall, first // 512 * 256 : first // 512 * 256 + 256].astype(BF)

        def write(lanes, value, i=i):
            out_ref[i, tall : tall + 8, lanes] = value

        put_small(write, bias_ref[...], gs[...])


def first_sum_kernel(y_ref, out_ref):
    count = y_ref.shape[0]
    total = y_ref[0].astype(F32)
    for i in range(1, count):
        total = total + y_ref[i].astype(F32)
    groups, tall = out_ref.shape[:2]
    bias, gain_rows = get_small(total[groups * tall : groups * tall + 8])
    small = jnp.concatenate([bias[:, 0:128], bias[:, 128:256], gain_rows, jnp.zeros((8, 128), F32)], axis=0)
    share = 32 // groups
    zeros = jnp.zeros((tall - 2 * share, 128), F32) if tall > 2 * share else None
    for j in range(groups):
        out_ref[j, :, 0:1024] = total[j * tall : j * tall + tall].astype(BF)
        part = small[j * share : j * share + share]
        high = part.astype(BF).astype(F32)
        pieces = [high, part - high] + ([] if zeros is None else [zeros])
        out_ref[j, :, 1024:1152] = jnp.concatenate(pieces, axis=0).astype(BF)


def second_sum_kernel(y_ref, out_ref):
    count = y_ref.shape[0]
    total = y_ref[0].astype(F32)
    for i in range(1, count):
        total = total + y_ref[i].astype(F32)
    groups, tall = out_ref.shape[:2]
    share = 32 // groups
    main = total[:, 0:1024].astype(BF)
    part = total[0:share, 1024:1152] + total[share : 2 * share, 1024:1152]
    high = part.astype(BF).astype(F32)
    pieces = [high, part - high] + ([jnp.zeros((tall - 2 * share, 128), F32)] if tall > 2 * share else [])
    side = jnp.concatenate(pieces, axis=0).astype(BF)
    for j in range(groups):
        out_ref[j, :, 0:1024] = main
        out_ref[j, :, 1024:1152] = side


def spread_kernel(y_ref, out_ref, small_ref):
    groups, tall = y_ref.shape[:2]
    small_ref[...] = y_ref[:, :, 1024:1152]
    for j in range(groups):
        part = y_ref[j, :, 0:1024]
        for i in range(out_ref.shape[0]):
            out_ref[i, j * tall : j * tall + tall] = part


def last_kernel(s_ref, mine_ref, theirs_ref, small_ref, other_ref, qkv_ref, proj_ref, small_out):
    @pl.when(s_ref[0] == 0)
    def _():
        for c, ref in ((0, mine_ref), (1, theirs_ref)):
            qkv_ref[:, c * 768 : c * 768 + 768] = ref[:, 0:768]
            for j in range(2):
                proj_ref[:, c * 512 + j * 256 : c * 512 + j * 256 + 256] = ref[j * 512 : j * 512 + 512, 768:1024]

    @pl.when(s_ref[0] != 0)
    def _():
        for c, ref in ((1, mine_ref), (0, theirs_ref)):
            qkv_ref[:, c * 768 : c * 768 + 768] = ref[:, 0:768]
            for j in range(2):
                proj_ref[:, c * 512 + j * 256 : c * 512 + j * 256 + 256] = ref[j * 512 : j * 512 + 512, 768:1024]

    groups = small_ref.shape[0]
    share = 32 // groups
    for j in range(groups):
        both = small_ref[j].astype(F32) + other_ref[j].astype(F32)
        small_out[j * share : j * share + share, :] = both[0:share] + both[share : 2 * share]


def call(kernel, outs, args, scratch=(), name=None, left=(), sems=0):
    def spec(i, a):
        space = pltpu.SMEM if a.dtype == jnp.int32 and a.ndim == 1 else pl.ANY if i in left else pltpu.VMEM
        return pl.BlockSpec(memory_space=space)

    specs = [spec(i, a) for i, a in enumerate(args)]
    return pl.pallas_call(
        kernel,
        out_shape=[jax.ShapeDtypeStruct(shape, kind) for shape, kind in outs],
        in_specs=specs,
        out_specs=[pl.BlockSpec(memory_space=pltpu.VMEM) for _ in outs],
        scratch_shapes=[pltpu.VMEM(shape, kind) for shape, kind in scratch] + ([pltpu.SemaphoreType.DMA((sems,))] if sems else []),
        compiler_params=pltpu.CompilerParams(vmem_limit_bytes=48 * 1024 * 1024),
        interpret=INTERPRET,
        name=name,
    )(*args)


def make_body(sizes):
    zl, nx_, zh, ny, nc = sizes
    rows, cols = zl * nx_, zh * ny * nc
    every = ("zl", "x", "zh", "y", "c")
    row_axes = ("zl", "x")
    col_axes = ("zh", "y")
    groups = zh * ny

    def row_pairs(value, first):
        pairs = []
        for low in range(first, rows - 1, 2):
            for j in range(cols):
                pairs += [(low * cols + j, (low + 1) * cols + j), ((low + 1) * cols + j, low * cols + j)]
        return lax.ppermute(value, every, pairs)

    def col_pairs(value, first):
        pairs = []
        for low in range(first, cols - 1, 2):
            for i in range(rows):
                pairs += [(i * cols + low, i * cols + low + 1), (i * cols + low + 1, i * cols + low)]
        return lax.ppermute(value, every, pairs)

    def swap(value):
        return lax.ppermute(value, "c", [(0, 1), (1, 0)])

    def body(image_feats, norm_gain, w_qkv, rel_bias, w_proj, out_grad):
        core = lax.axis_index("c")
        row_anchor = (lax.axis_index("zl") * nx_ + lax.axis_index("x")) * 7
        col_anchor = ((lax.axis_index("zh") * ny + lax.axis_index("y")) * nc + core) * 7
        scalars = jnp.stack([core, row_anchor, col_anchor, jnp.int32(rows * 7), jnp.int32(cols * 7), (row_anchor // 7) % 2]).astype(jnp.int32)
        gain = norm_gain.reshape(1, 1024)
        pick = jnp.asarray(PICK, BF)
        perm = jnp.asarray(PERM, BF)
        rel = jnp.pad(rel_bias, ((0, 0), (0, 3), (0, 3))).reshape(8, 256)
        queries, own_kv, attn_grad, m1, normed, og_keep, normal_x, inv_std, row_a, row_b = call(
            front_kernel,
            [((3, 64, 512), BF), ((3, 64, 1024), BF), ((3, 64, 512), BF), ((192, 1536), BF), ((192, 1024), BF), ((192, 512), BF), ((192, 1024), F32), ((192, 128), F32), ((3, 24, 1024), BF), ((3, 24, 1024), BF)],
            [scalars, image_feats, out_grad, gain, w_qkv, w_proj],
            [((192, 1024), F32), ((192, 1024), F32), ((3, 7, 7, 1024), BF), ((3, 7, 7, 1024), BF), ((1024, 1536), BF), ((512, 1024), BF)],
            "front",
            (1, 2, 4, 5),
            4,
        )
        row_a = row_pairs(row_a, 0)
        row_b = row_pairs(row_b, 1)
        (table,) = call(
            table_kernel,
            [((512, 256), F32)],
            [scalars, rel, jnp.asarray(KEY_ROW), jnp.asarray(KEY_COL), perm],
            [((2, 512, 128), F32)],
            "table",
        )
        edges, col_a, col_b = call(
            columns_kernel,
            [((3, 64, 1024), BF), ((3, 48, 1024), BF), ((3, 48, 1024), BF)],
            [scalars, own_kv, row_a, row_b, pick],
            [((3, 128, 1024), BF)],
            "columns",
        )
        col_a = col_pairs(col_a, 0)
        col_b = col_pairs(col_b, 1)
        attended, query_grad, own_grad, col_a, col_b, score_sum = call(
            attention_kernel,
            [((3, 64, 512), BF), ((3, 64, 512), BF), ((3, 128, 1024), F32), ((3, 48, 1024), BF), ((3, 48, 1024), BF), ((512, 256), F32)],
            [scalars, queries, own_kv, edges, col_a, col_b, attn_grad, table],
            [((3, 256, 1024), BF), ((3, 96, 1024), BF)],
            "attention",
        )
        col_a = col_pairs(col_a, 0)
        col_b = col_pairs(col_b, 1)
        m1_other = swap(m1)
        layer_out, bias_part = call(
            out_kernel,
            [((3, 7, 7, 1024), BF), ((8, 256), F32)],
            [attended, w_proj, image_feats, score_sum, perm],
            [((192, 1024), F32), ((2, 512, 128), F32)],
            "layer_out",
        )
        own_sum, row_a, row_b = call(
            edges_kernel,
            [((3, 64, 1024), F32), ((3, 24, 1024), BF), ((3, 24, 1024), BF)],
            [scalars, own_grad, pick, col_a, col_b],
            [((3, 96, 1024), BF)],
            "edges",
        )
        row_a = row_pairs(row_a, 0)
        row_b = row_pairs(row_b, 1)
        dqkv, m2 = call(
            join_kernel,
            [((192, 1536), BF), ((192, 1280), BF)],
            [scalars, own_sum, query_grad, attended, row_a, row_b, bias_part],
            [((3, 64, 1024), F32)],
            "join",
        )
        m2_other = swap(m2)
        feats_grad, gain_part = call(
            feats_kernel,
            [((3, 7, 7, 1024), BF), ((1, 1024), F32)],
            [dqkv, w_qkv, normal_x, inv_std, gain, out_grad],
            [((192, 1024), F32)],
            "feats",
        )
        tall1 = 1024 // rows
        tall2 = tall1 // groups
        (send,) = call(
            weights_kernel,
            [((rows, tall1 + 8, 1024), BF)],
            [scalars, normed, attended, dqkv, og_keep, m1_other, m2_other, gain_part, bias_part],
            [((1024, 768), F32), ((512, 512), F32), ((8, 128), F32)],
            "weights",
        )
        send = lax.all_to_all(send, row_axes, 0, 0, tiled=True)
        (send,) = call(first_sum_kernel, [((groups, tall2, 1152), BF)], [send], (), "first_sum")
        send = lax.all_to_all(send, col_axes, 0, 0, tiled=True)
        (send,) = call(second_sum_kernel, [((groups, tall2, 1152), BF)], [send], (), "second_sum")
        send = lax.all_to_all(send, col_axes, 0, 0, tiled=True)
        send, small = call(spread_kernel, [((rows, tall1, 1024), BF), ((groups, tall2, 128), BF)], [send], (), "spread")
        small_other = swap(small)
        mine = lax.all_to_all(send, row_axes, 0, 0, tiled=True).reshape(1024, 1024)
        theirs = swap(mine)
        qkv_grad, proj_grad, small = call(
            last_kernel,
            [((1024, 1536), BF), ((512, 1024), BF), ((32, 128), F32)],
            [scalars, mine, theirs, small, small_other],
            (),
            "last",
        )
        gain_grad = small[16:24].reshape(1024)
        bias_grad = jnp.concatenate([small[0:8], small[8:16]], axis=1).reshape(8, 16, 16)[:, :13, :13]
        return (layer_out, feats_grad, qkv_grad, proj_grad, gain_grad, bias_grad)

    return body


def solution(mesh, sizes=(2, 4, 4, 4, 2)):
    fine = Mesh(mesh.devices.reshape(sizes), ("zl", "x", "zh", "y", "c"))
    image = P(None, ("zl", "x"), ("zh", "y", "c"), None)
    return jax.shard_map(
        make_body(sizes),
        mesh=fine,
        in_specs=(image, P(), P(), P(), P(), image),
        out_specs=(image, image, P(), P(), P(), P()),
        check_vma=False,
    )
```

```python
import numpy as np
import jax
import jax.numpy as jnp
from jax import lax
from jax.experimental import pallas as pl
from jax.experimental.pallas import tpu as pltpu
from jax.sharding import Mesh
from jax.sharding import PartitionSpec as P

WIN = 7
EPS = 1e-05
BF = jnp.bfloat16
F32 = jnp.float32
INTERPRET = False

UP, DN, LF, RT = 64, 96, 128, 176


def tables():
    key_row = np.full((1, 256), -100, np.int32)
    key_col = np.full((1, 256), -100, np.int32)
    for r in range(7):
        for c in range(7):
            key_row[0, 8 * r + c] = r
            key_col[0, 8 * r + c] = c
    for s in range(3):
        for c in range(7):
            for slot, row in ((UP, s - 3), (DN, 7 + s)):
                key_row[0, slot + 8 * s + c] = row
                key_col[0, slot + 8 * s + c] = c
        for r in range(13):
            for slot, col in ((LF, s - 3), (RT, 7 + s)):
                key_row[0, slot + 16 * s + r] = r - 3
                key_col[0, slot + 16 * s + r] = col
    perm = np.zeros((256, 256), np.float32)
    for slot in range(256):
        if key_row[0, slot] > -100:
            perm[(key_row[0, slot] + 3) * 16 + key_col[0, slot] + 3, slot] = 1
    pick = np.zeros((96, 128), np.float32)
    for s in range(3):
        for r in range(13):
            row = r - 3
            start = UP + 8 * r if row < 0 else (DN + 8 * (row - 7) if row > 6 else 8 * row)
            pick[16 * s + r, start + s] = 1
            pick[48 + 16 * s + r, start + 4 + s] = 1
    return key_row, key_col, perm, pick


KEY_ROW, KEY_COL, PERM, PICK = tables()


def nn(a, b):
    return lax.dot_general(a, b, (((1,), (0,)), ((), ())), preferred_element_type=F32)


def nt(a, b):
    return lax.dot_general(a, b, (((1,), (1,)), ((), ())), preferred_element_type=F32)


def tn(a, b):
    return lax.dot_general(a, b, (((0,), (0,)), ((), ())), preferred_element_type=F32)


def three_parts(x):
    high = x.astype(BF)
    rest = x - high.astype(F32)
    mid = rest.astype(BF)
    low = (rest - mid.astype(F32)).astype(BF)
    return high, mid, low


def front_kernel(s_ref, x_hbm, og_hbm, gain_hbm, wqkv_hbm, wproj_hbm, q_ref, kv_ref, ag_ref, m1_hbm, nb_ref, ogk_ref, nx_ref, inv_ref, a_ref, b_ref, xs, os, x_ref, og_ref, gain_ref, wqkv_ref, wproj_ref, m1_ref, sems):
    loads = [
        pltpu.make_async_copy(source, target, sems.at[i])
        for i, (source, target) in enumerate(((x_hbm, x_ref), (og_hbm, og_ref), (wqkv_hbm, wqkv_ref), (wproj_hbm, wproj_ref), (gain_hbm, gain_ref)))
    ]
    for load in loads:
        load.start()
    xs[...] = jnp.zeros_like(xs)
    os[...] = jnp.zeros_like(os)
    loads[0].wait()
    for t in range(3):
        for r in range(7):
            xs[t * 64 + r * 8 : t * 64 + r * 8 + 7, :] = x_ref[t, r].astype(F32)
    xf = xs[...]
    dev = xf - jnp.mean(xf, axis=-1, keepdims=True)
    inv = lax.rsqrt(jnp.mean(dev * dev, axis=-1, keepdims=True) + EPS)
    nx = dev * inv
    loads[4].wait()
    nx_ref[...] = nx
    inv_ref[...] = jnp.broadcast_to(inv, inv_ref.shape)
    normed = (nx * gain_ref[...]).astype(BF)
    nb_ref[...] = normed
    m1_ref[:, :1024] = normed
    sends = [pltpu.make_async_copy(m1_ref.at[:, lanes], m1_hbm.at[:, lanes], sems.at[5 + i]) for i, lanes in enumerate((slice(0, 1024), slice(1024, 1536)))]
    sends[0].start()
    loads[2].wait()
    qkv = nn(normed, wqkv_ref[...]).astype(BF)
    for t in range(3):
        rows = qkv[t * 64 : t * 64 + 64]
        q_ref[t] = rows[:, :512]
        kv_ref[t] = rows[:, 512:]

    @pl.when(s_ref[5] == 0)
    def _():
        for t in range(3):
            a_ref[t] = kv_ref[t, 32:56]
            b_ref[t] = kv_ref[t, 0:24]

    @pl.when(s_ref[5] != 0)
    def _():
        for t in range(3):
            a_ref[t] = kv_ref[t, 0:24]
            b_ref[t] = kv_ref[t, 32:56]

    loads[1].wait()
    for t in range(3):
        for r in range(7):
            os[t * 64 + r * 8 : t * 64 + r * 8 + 7, :] = og_ref[t, r].astype(F32)
    og = os[...].astype(BF)
    loads[3].wait()

    @pl.when(s_ref[0] == 0)
    def _():
        ogk_ref[...] = og[:, :512]
        m1_ref[:, 1024:] = og[:, 512:]

    @pl.when(s_ref[0] != 0)
    def _():
        ogk_ref[...] = og[:, 512:]
        m1_ref[:, 1024:] = og[:, :512]

    sends[1].start()
    ag_ref[...] = nt(og, wproj_ref[...]).astype(BF).reshape(3, 64, 512)
    sends[0].wait()
    sends[1].wait()


def columns_kernel(s_ref, kv_ref, got_a, got_b, pick_ref, edge_ref, a_ref, b_ref, rows):
    edge_ref[...] = jnp.zeros_like(edge_ref)

    @pl.when(s_ref[5] == 0)
    def _():
        for t in range(3):
            edge_ref[t, 0:24] = got_b[t]
            edge_ref[t, 32:56] = got_a[t]

    @pl.when(s_ref[5] != 0)
    def _():
        for t in range(3):
            edge_ref[t, 0:24] = got_a[t]
            edge_ref[t, 32:56] = got_b[t]

    for t in range(3):
        rows[t, 0:64] = kv_ref[t]
        rows[t, 64:128] = edge_ref[t]
    outs = [nn(pick_ref[...], rows[t]).astype(BF) for t in range(3)]

    @pl.when(s_ref[0] == 0)
    def _():
        for t in range(3):
            a_ref[t] = outs[t][48:96]
            b_ref[t] = outs[t][0:48]

    @pl.when(s_ref[0] != 0)
    def _():
        for t in range(3):
            a_ref[t] = outs[t][0:48]
            b_ref[t] = outs[t][48:96]


def table_kernel(s_ref, rel_ref, key_row_ref, key_col_ref, perm_ref, out_ref, grid_ref):
    grid_ref[...] = jnp.zeros_like(grid_ref)
    line = rel_ref[...]
    for r in range(7):
        for c in range(7):
            turned = pltpu.roll(line, ((r - 3) * 16 + c - 3) % 256, 1)
            for half in range(2):
                grid_ref.at[half][pl.ds(r * 8 + c, 8, stride=64), :] = turned[:, half * 128 : half * 128 + 128]
    high, mid, low = three_parts(jnp.concatenate([grid_ref[0], grid_ref[1]], axis=1))
    perm = perm_ref[...]
    table = nn(high, perm) + (nn(mid, perm) + nn(low, perm))
    place = lax.broadcasted_iota(jnp.int32, (64, 256), 0)
    row = place // 8
    col = place % 8
    row_first = jnp.clip(s_ref[1] + row - 3, 0, s_ref[3] - WIN) - s_ref[1]
    col_first = jnp.clip(s_ref[2] + col - 3, 0, s_ref[4] - WIN) - s_ref[2]
    key_row = key_row_ref[...]
    key_col = key_col_ref[...]
    valid = (key_row >= row_first) & (key_row < row_first + WIN) & (key_col >= col_first) & (key_col < col_first + WIN) & (row < 7) & (col < 7)
    for h in range(8):
        out_ref[h * 64 : h * 64 + 64, :] = jnp.where(valid, table[h * 64 : h * 64 + 64], -1e30)


def attention_kernel(s_ref, q_ref, kv_ref, edge_ref, got_a, got_b, ag_ref, table_ref, att_ref, dq_ref, own_ref, a_ref, b_ref, g_ref, keys, dkv):
    keys[:, 224:256, :] = jnp.zeros((3, 32, 1024), BF)
    for t in range(3):
        keys[t, 0:64] = kv_ref[t]
        keys[t, 64:128] = edge_ref[t]

    @pl.when(s_ref[0] == 0)
    def _():
        for t in range(3):
            keys[t, LF : LF + 48] = got_b[t]
            keys[t, RT : RT + 48] = got_a[t]

    @pl.when(s_ref[0] != 0)
    def _():
        for t in range(3):
            keys[t, LF : LF + 48] = got_a[t]
            keys[t, RT : RT + 48] = got_b[t]

    at_row = lax.broadcasted_iota(jnp.int32, (256, 256), 0) // 64
    at_col = lax.broadcasted_iota(jnp.int32, (256, 256), 1) // 64
    diag = at_row == at_col

    def spread(x):
        x = x.astype(F32)
        return jnp.where(diag, jnp.concatenate([x, x, x, x], axis=0), 0.0).astype(BF)

    def gather(x):
        x = jnp.where(diag, x, 0.0)
        return (x[0:64] + x[64:128]) + (x[128:192] + x[192:256])

    totals = [None, None]
    for t in range(3):
        for g in range(2):
            at = slice(g * 256, g * 256 + 256)
            k = keys[t, :, g * 256 : g * 256 + 256]
            v = keys[t, :, 512 + g * 256 : 768 + g * 256]
            qb = spread(q_ref[t, :, at])
            db = spread(ag_ref[t, :, at])
            scores = nt(qb, k) * 0.125 + table_ref[at, :]
            terms = jnp.exp(scores - jnp.max(scores, axis=-1, keepdims=True))
            probs = terms / jnp.sum(terms, axis=-1, keepdims=True)
            low = probs.astype(BF)
            att_ref[t, :, at] = gather(nn(low, v)).astype(BF)
            dprobs = nt(db, v)
            dscores = probs * (dprobs - jnp.sum(probs * dprobs, axis=-1, keepdims=True))
            totals[g] = dscores if t == 0 else totals[g] + dscores
            dlow = dscores.astype(BF)
            dq_ref[t, :, at] = (gather(nn(dlow, k)) * 0.125).astype(BF)
            for lanes, grad in ((at, tn(dlow, qb) * 0.125), (slice(512 + g * 256, 768 + g * 256), tn(low, db))):
                own_ref[t, :, lanes] = grad[0:128]
                dkv[t, :, lanes] = grad[128:224].astype(BF)

    @pl.when(s_ref[0] == 0)
    def _():
        for t in range(3):
            a_ref[t] = dkv[t, 48:96]
            b_ref[t] = dkv[t, 0:48]

    @pl.when(s_ref[0] != 0)
    def _():
        for t in range(3):
            a_ref[t] = dkv[t, 0:48]
            b_ref[t] = dkv[t, 48:96]

    g_ref[0:256] = totals[0]
    g_ref[256:512] = totals[1]


def out_kernel(att_ref, wproj_ref, x_ref, g_ref, perm_ref, out_ref, bias_ref, ys, gs):
    ys[...] = nn(att_ref[...].reshape(192, 512), wproj_ref[...])
    for t in range(3):
        for r in range(7):
            out_ref[t, r] = (x_ref[t, r].astype(F32) + ys[t * 64 + r * 8 : t * 64 + r * 8 + 7, :]).astype(BF)
    high, mid, low = three_parts(g_ref[...])
    perm = perm_ref[...]
    grid = nt(high, perm) + (nt(mid, perm) + nt(low, perm))
    for half in range(2):
        gs[half] = grid[:, half * 128 : half * 128 + 128]
    total = None
    for r in range(7):
        for c in range(7):
            part = jnp.concatenate([gs.at[half][pl.ds(r * 8 + c, 8, stride=64), :] for half in range(2)], axis=1)
            part = pltpu.roll(part, ((3 - r) * 16 + 3 - c) % 256, 1)
            total = part if total is None else total + part
    bias_ref[...] = total


def edges_kernel(s_ref, own_ref, pick_ref, got_a, got_b, sum_ref, a_ref, b_ref, side):
    @pl.when(s_ref[0] == 0)
    def _():
        for t in range(3):
            side[t, 0:48] = got_b[t]
            side[t, 48:96] = got_a[t]

    @pl.when(s_ref[0] != 0)
    def _():
        for t in range(3):
            side[t, 0:48] = got_a[t]
            side[t, 48:96] = got_b[t]

    totals = [own_ref[t] + tn(pick_ref[...], side[t]) for t in range(3)]
    for t in range(3):
        sum_ref[t] = totals[t][0:64]

    @pl.when(s_ref[5] == 0)
    def _():
        for t in range(3):
            a_ref[t] = totals[t][96:120].astype(BF)
            b_ref[t] = totals[t][64:88].astype(BF)

    @pl.when(s_ref[5] != 0)
    def _():
        for t in range(3):
            a_ref[t] = totals[t][64:88].astype(BF)
            b_ref[t] = totals[t][96:120].astype(BF)


def join_kernel(s_ref, sum_ref, dq_ref, att_ref, got_a, got_b, bias_ref, dqkv_ref, m2_ref, acc):
    acc[...] = sum_ref[...]

    @pl.when(s_ref[5] == 0)
    def _():
        for t in range(3):
            acc[t, 32:56] = acc[t, 32:56] + got_a[t].astype(F32)
            acc[t, 0:24] = acc[t, 0:24] + got_b[t].astype(F32)

    @pl.when(s_ref[5] != 0)
    def _():
        for t in range(3):
            acc[t, 0:24] = acc[t, 0:24] + got_a[t].astype(F32)
            acc[t, 32:56] = acc[t, 32:56] + got_b[t].astype(F32)

    for t in range(3):
        dqkv_ref[t * 64 : t * 64 + 64, 0:512] = dq_ref[t]
        dqkv_ref[t * 64 : t * 64 + 64, 512:1536] = acc[t].astype(BF)
    m2_ref[:, 0:512] = att_ref[...].reshape(192, 512)

    @pl.when(s_ref[0] == 0)
    def _():
        m2_ref[:, 512:1280] = dqkv_ref[:, 768:1536]

    @pl.when(s_ref[0] != 0)
    def _():
        m2_ref[:, 512:1280] = dqkv_ref[:, 0:768]


def feats_kernel(dqkv_ref, wqkv_ref, nx_ref, inv_ref, gain_ref, og_ref, out_ref, gg_ref, ys):
    ngrad = nt(dqkv_ref[...], wqkv_ref[...])
    nx = nx_ref[...]
    gg_ref[...] = jnp.sum(ngrad * nx, axis=0, keepdims=True)
    scaled = ngrad * gain_ref[...]
    correction = scaled - jnp.mean(scaled, axis=-1, keepdims=True) - nx * jnp.mean(scaled * nx, axis=-1, keepdims=True)
    ys[...] = inv_ref[:, 0:1] * correction
    for t in range(3):
        for r in range(7):
            out_ref[t, r] = (og_ref[t, r].astype(F32) + ys[t * 64 + r * 8 : t * 64 + r * 8 + 7, :]).astype(BF)


def put_small(write, bias, gain_rows):
    high = bias.astype(BF)
    write(slice(0, 256), high)
    write(slice(256, 512), (bias - high.astype(F32)).astype(BF))
    high = gain_rows.astype(BF)
    write(slice(512, 640), high)
    write(slice(640, 768), (gain_rows - high.astype(F32)).astype(BF))
    write(slice(768, 1024), jnp.zeros((8, 256), BF))


def get_small(block):
    return block[:, 0:256] + block[:, 256:512], block[:, 512:640] + block[:, 640:768]


def weights_kernel(s_ref, nb_ref, att_ref, dqkv_ref, ogk_ref, m1_ref, m2_ref, gg_ref, bias_ref, out_ref, zq, zp, gs):
    count = out_ref.shape[0]
    tall = 1024 // count

    @pl.when(s_ref[0] == 0)
    def _():
        zq[...] = tn(nb_ref[...], dqkv_ref[:, 0:768]) + tn(m1_ref[:, 0:1024], m2_ref[:, 512:1280])

    @pl.when(s_ref[0] != 0)
    def _():
        zq[...] = tn(nb_ref[...], dqkv_ref[:, 768:1536]) + tn(m1_ref[:, 0:1024], m2_ref[:, 512:1280])

    zp[...] = tn(att_ref[...].reshape(192, 512), ogk_ref[...]) + tn(m2_ref[:, 0:512], m1_ref[:, 1024:1536])
    for j in range(8):
        gs[j : j + 1, :] = gg_ref[:, j * 128 : j * 128 + 128]
    for i in range(count):
        out_ref[i, 0:tall, 0:768] = zq[i * tall : i * tall + tall].astype(BF)
        first = i * tall
        out_ref[i, 0:tall, 768:1024] = zp[first % 512 : first % 512 + tall, first // 512 * 256 : first // 512 * 256 + 256].astype(BF)

        def write(lanes, value, i=i):
            out_ref[i, tall : tall + 8, lanes] = value

        put_small(write, bias_ref[...], gs[...])


def axis_sum_kernel(y_ref, out_ref):
    count = y_ref.shape[0]
    total = y_ref[0].astype(F32)
    for i in range(1, count):
        total = total + y_ref[i].astype(F32)
    groups = out_ref.shape[0]
    tall = out_ref.shape[1] - 8
    bias, gain_rows = get_small(total[groups * tall : groups * tall + 8])
    for j in range(groups):
        out_ref[j, 0:tall] = total[j * tall : j * tall + tall].astype(BF)

        def write(lanes, value, j=j):
            out_ref[j, tall : tall + 8, lanes] = value

        put_small(write, bias, gain_rows)


def first_sum_kernel(y_ref, out_ref):
    count = y_ref.shape[0]
    total = y_ref[0].astype(F32)
    for i in range(1, count):
        total = total + y_ref[i].astype(F32)
    groups, tall = out_ref.shape[:2]
    bias, gain_rows = get_small(total[groups * tall : groups * tall + 8])
    small = jnp.concatenate([bias[:, 0:128], bias[:, 128:256], gain_rows, jnp.zeros((8, 128), F32)], axis=0)
    share = 32 // groups
    zeros = jnp.zeros((tall - 2 * share, 128), F32) if tall > 2 * share else None
    for j in range(groups):
        out_ref[j, :, 0:1024] = total[j * tall : j * tall + tall].astype(BF)
        part = small[j * share : j * share + share]
        high = part.astype(BF).astype(F32)
        pieces = [high, part - high] + ([] if zeros is None else [zeros])
        out_ref[j, :, 1024:1152] = jnp.concatenate(pieces, axis=0).astype(BF)


def second_sum_kernel(y_ref, out_ref):
    count = y_ref.shape[0]
    total = y_ref[0].astype(F32)
    for i in range(1, count):
        total = total + y_ref[i].astype(F32)
    groups, tall = out_ref.shape[:2]
    share = 32 // groups
    main = total[:, 0:1024].astype(BF)
    part = total[0:share, 1024:1152] + total[share : 2 * share, 1024:1152]
    high = part.astype(BF).astype(F32)
    pieces = [high, part - high] + ([jnp.zeros((tall - 2 * share, 128), F32)] if tall > 2 * share else [])
    side = jnp.concatenate(pieces, axis=0).astype(BF)
    for j in range(groups):
        out_ref[j, :, 0:1024] = main
        out_ref[j, :, 1024:1152] = side


def spread_kernel(y_ref, out_ref, small_ref):
    groups, tall = y_ref.shape[:2]
    small_ref[...] = y_ref[:, :, 1024:1152]
    for j in range(groups):
        part = y_ref[j, :, 0:1024]
        for i in range(out_ref.shape[0]):
            out_ref[i, j * tall : j * tall + tall] = part


def small_kernel(small_ref, other_ref, out_ref):
    groups = small_ref.shape[0]
    share = 32 // groups
    for j in range(groups):
        both = small_ref[j].astype(F32) + other_ref[j].astype(F32)
        out_ref[j * share : j * share + share, :] = both[0:share] + both[share : 2 * share]


def place(c, ref, qkv_ref, proj_ref, sems):
    copies = [pltpu.make_async_copy(ref.at[:, 0:768], qkv_ref.at[:, c * 768 : c * 768 + 768], sems.at[0])]
    for j in range(2):
        copies.append(pltpu.make_async_copy(ref.at[j * 512 : j * 512 + 512, 768:1024], proj_ref.at[:, c * 512 + j * 256 : c * 512 + j * 256 + 256], sems.at[1 + j]))
    for copy in copies:
        copy.start()
    for copy in copies:
        copy.wait()


def mine_kernel(s_ref, mine_ref, qkv_ref, proj_ref, sems):
    @pl.when(s_ref[0] == 0)
    def _():
        place(0, mine_ref, qkv_ref, proj_ref, sems)

    @pl.when(s_ref[0] != 0)
    def _():
        place(1, mine_ref, qkv_ref, proj_ref, sems)


def theirs_kernel(s_ref, theirs_ref, qkv_in, proj_in, qkv_ref, proj_ref, sems):
    @pl.when(s_ref[0] == 0)
    def _():
        place(1, theirs_ref, qkv_ref, proj_ref, sems)

    @pl.when(s_ref[0] != 0)
    def _():
        place(0, theirs_ref, qkv_ref, proj_ref, sems)


def call(kernel, outs, args, scratch=(), name=None, left=(), sems=0, outs_left=(), aliases=None):
    def spec(i, a):
        space = pltpu.SMEM if a.dtype == jnp.int32 and a.ndim == 1 else pltpu.HBM if i in left else pltpu.VMEM
        return pl.BlockSpec(memory_space=space)

    specs = [spec(i, a) for i, a in enumerate(args)]
    args = [pltpu.with_memory_space_constraint(a, pltpu.HBM) if i in left and not INTERPRET else a for i, a in enumerate(args)]
    return pl.pallas_call(
        kernel,
        out_shape=[jax.ShapeDtypeStruct(shape, kind) for shape, kind in outs],
        in_specs=specs,
        out_specs=[pl.BlockSpec(memory_space=pltpu.HBM if i in outs_left else pltpu.VMEM) for i in range(len(outs))],
        input_output_aliases=aliases or {},
        scratch_shapes=[pltpu.VMEM(shape, kind) for shape, kind in scratch] + ([pltpu.SemaphoreType.DMA((sems,))] if sems else []),
        compiler_params=pltpu.CompilerParams(vmem_limit_bytes=48 * 1024 * 1024),
        interpret=INTERPRET,
        name=name,
    )(*args)


def make_body(sizes):
    zl, nx_, zh, ny, nc = sizes
    rows, cols = zl * nx_, zh * ny * nc
    every = ("zl", "x", "zh", "y", "c")
    deep = zl * zh
    ids = np.arange(rows * cols).reshape(sizes)
    along_x = [[[int(v) for v in ids[a, :, b, k, c]] for a in range(zl) for b in range(zh) for k in range(ny)] for c in range(nc)]
    along_y = [[[int(v) for v in ids[a, k, b, :, c]] for a in range(zl) for b in range(zh) for k in range(nx_)] for c in range(nc)]
    first_groups = along_x[0] + along_y[1]
    second_groups = along_y[0] + along_x[1]
    assert nx_ == ny and nc == 2

    def row_pairs(value, first):
        pairs = []
        for low in range(first, rows - 1, 2):
            for j in range(cols):
                pairs += [(low * cols + j, (low + 1) * cols + j), ((low + 1) * cols + j, low * cols + j)]
        return lax.ppermute(value, every, pairs)

    def col_pairs(value, first):
        pairs = []
        for low in range(first, cols - 1, 2):
            for i in range(rows):
                pairs += [(i * cols + low, i * cols + low + 1), (i * cols + low + 1, i * cols + low)]
        return lax.ppermute(value, every, pairs)

    def trade(value, groups):
        return lax.all_to_all(value, every, 0, 0, tiled=True, axis_index_groups=groups)

    def trade_deep(value):
        return lax.all_to_all(value, ("zl", "zh"), 0, 0, tiled=True)

    def swap(value):
        return lax.ppermute(value, "c", [(0, 1), (1, 0)])

    def body(image_feats, norm_gain, w_qkv, rel_bias, w_proj, out_grad):
        core = lax.axis_index("c")
        row_anchor = (lax.axis_index("zl") * nx_ + lax.axis_index("x")) * 7
        col_anchor = ((lax.axis_index("zh") * ny + lax.axis_index("y")) * nc + core) * 7
        scalars = jnp.stack([core, row_anchor, col_anchor, jnp.int32(rows * 7), jnp.int32(cols * 7), (row_anchor // 7) % 2]).astype(jnp.int32)
        gain = norm_gain.reshape(1, 1024)
        pick = jnp.asarray(PICK, BF)
        perm = jnp.asarray(PERM, BF)
        rel = jnp.pad(rel_bias, ((0, 0), (0, 3), (0, 3))).reshape(8, 256)
        queries, own_kv, attn_grad, m1, normed, og_keep, normal_x, inv_std, row_a, row_b = call(
            front_kernel,
            [((3, 64, 512), BF), ((3, 64, 1024), BF), ((3, 64, 512), BF), ((192, 1536), BF), ((192, 1024), BF), ((192, 512), BF), ((192, 1024), F32), ((192, 128), F32), ((3, 24, 1024), BF), ((3, 24, 1024), BF)],
            [scalars, image_feats, out_grad, gain, w_qkv, w_proj],
            [((192, 1024), F32), ((192, 1024), F32), ((3, 7, 7, 1024), BF), ((3, 7, 7, 1024), BF), ((1, 1024), F32), ((1024, 1536), BF), ((512, 1024), BF), ((192, 1536), BF)],
            "front",
            (1, 2, 3, 4, 5),
            7,
            (3,),
        )
        row_b = row_pairs(row_b, 1)
        row_a = row_pairs(row_a, 0)
        (table,) = call(
            table_kernel,
            [((512, 256), F32)],
            [scalars, rel, jnp.asarray(KEY_ROW), jnp.asarray(KEY_COL), perm],
            [((2, 512, 128), F32)],
            "table",
        )
        edges, col_a, col_b = call(
            columns_kernel,
            [((3, 64, 1024), BF), ((3, 48, 1024), BF), ((3, 48, 1024), BF)],
            [scalars, own_kv, row_a, row_b, pick],
            [((3, 128, 1024), BF)],
            "columns",
        )
        col_b = col_pairs(col_b, 1)
        col_a = col_pairs(col_a, 0)
        attended, query_grad, own_grad, col_a, col_b, score_sum = call(
            attention_kernel,
            [((3, 64, 512), BF), ((3, 64, 512), BF), ((3, 128, 1024), F32), ((3, 48, 1024), BF), ((3, 48, 1024), BF), ((512, 256), F32)],
            [scalars, queries, own_kv, edges, col_a, col_b, attn_grad, table],
            [((3, 256, 1024), BF), ((3, 96, 1024), BF)],
            "attention",
        )
        col_b = col_pairs(col_b, 1)
        col_a = col_pairs(col_a, 0)
        m1_other = swap(m1)
        layer_out, bias_part = call(
            out_kernel,
            [((3, 7, 7, 1024), BF), ((8, 256), F32)],
            [attended, w_proj, image_feats, score_sum, perm],
            [((192, 1024), F32), ((2, 512, 128), F32)],
            "layer_out",
        )
        own_sum, row_a, row_b = call(
            edges_kernel,
            [((3, 64, 1024), F32), ((3, 24, 1024), BF), ((3, 24, 1024), BF)],
            [scalars, own_grad, pick, col_a, col_b],
            [((3, 96, 1024), BF)],
            "edges",
        )
        row_b = row_pairs(row_b, 1)
        row_a = row_pairs(row_a, 0)
        dqkv, m2 = call(
            join_kernel,
            [((192, 1536), BF), ((192, 1280), BF)],
            [scalars, own_sum, query_grad, attended, row_a, row_b, bias_part],
            [((3, 64, 1024), F32)],
            "join",
        )
        m2_other = swap(m2)
        feats_grad, gain_part = call(
            feats_kernel,
            [((3, 7, 7, 1024), BF), ((1, 1024), F32)],
            [dqkv, w_qkv, normal_x, inv_std, gain, out_grad],
            [((192, 1024), F32)],
            "feats",
        )
        tall1 = 1024 // nx_
        tall2 = tall1 // ny
        tall3 = tall2 // deep
        (send,) = call(
            weights_kernel,
            [((nx_, tall1 + 8, 1024), BF)],
            [scalars, normed, attended, dqkv, og_keep, m1_other, m2_other, gain_part, bias_part],
            [((1024, 768), F32), ((512, 512), F32), ((8, 128), F32)],
            "weights",
        )
        send = trade(send, first_groups)
        (send,) = call(axis_sum_kernel, [((ny, tall2 + 8, 1024), BF)], [send], (), "first_sum")
        send = trade(send, second_groups)
        (send,) = call(first_sum_kernel, [((deep, tall3, 1152), BF)], [send], (), "second_sum")
        send = trade_deep(send)
        (send,) = call(second_sum_kernel, [((deep, tall3, 1152), BF)], [send], (), "third_sum")
        send = trade_deep(send)
        send, small = call(spread_kernel, [((ny, tall2, 1024), BF), ((deep, tall3, 128), BF)], [send], (), "spread")
        small_other = swap(small)
        send = trade(send, second_groups).reshape(1, tall1, 1024)
        mine = trade(jnp.broadcast_to(send, (nx_, tall1, 1024)), first_groups).reshape(1024, 1024)
        theirs = swap(mine)
        weight_outs = [((1024, 1536), BF), ((512, 1024), BF)]
        (small,) = call(small_kernel, [((32, 128), F32)], [small, small_other], (), "small")
        qkv_grad, proj_grad = call(mine_kernel, weight_outs, [scalars, mine], (), "mine", (1,), 3, (0, 1))
        qkv_grad, proj_grad = call(theirs_kernel, weight_outs, [scalars, theirs, qkv_grad, proj_grad], (), "theirs", (1, 2, 3), 3, (0, 1), {2: 0, 3: 1})
        gain_grad = small[16:24].reshape(1024)
        bias_grad = jnp.concatenate([small[0:8], small[8:16]], axis=1).reshape(8, 16, 16)[:, :13, :13]
        return (layer_out, feats_grad, qkv_grad, proj_grad, gain_grad, bias_grad)

    return body


def solution(mesh, sizes=(2, 4, 4, 4, 2)):
    fine = Mesh(mesh.devices.reshape(sizes), ("zl", "x", "zh", "y", "c"))
    image = P(None, ("zl", "x"), ("zh", "y", "c"), None)
    return jax.shard_map(
        make_body(sizes),
        mesh=fine,
        in_specs=(image, P(), P(), P(), P(), image),
        out_specs=(image, image, P(), P(), P(), P()),
        check_vma=False,
    )
```

```python
import numpy as np
import jax
import jax.numpy as jnp
from jax import lax
from jax.experimental import pallas as pl
from jax.experimental.pallas import tpu as pltpu
from jax.sharding import Mesh
from jax.sharding import PartitionSpec as P

WIN = 7
EPS = 1e-05
BF = jnp.bfloat16
F32 = jnp.float32
INTERPRET = False

UP, DN, LF, RT = 64, 96, 128, 176
HIGH = 13


def tables():
    key_row = np.full((1, 256), -100, np.int32)
    key_col = np.full((1, 256), -100, np.int32)
    for r in range(7):
        for c in range(7):
            key_row[0, 8 * r + c] = r
            key_col[0, 8 * r + c] = c
    for s in range(3):
        for c in range(7):
            for slot, row in ((UP, s - 3), (DN, 7 + s)):
                key_row[0, slot + 8 * s + c] = row
                key_col[0, slot + 8 * s + c] = c
        for r in range(13):
            for slot, col in ((LF, s - 3), (RT, 7 + s)):
                key_row[0, slot + HIGH * s + r] = r - 3
                key_col[0, slot + HIGH * s + r] = col
    perm = np.zeros((256, 256), np.float32)
    for slot in range(256):
        if key_row[0, slot] > -100:
            perm[(key_row[0, slot] + 3) * 16 + key_col[0, slot] + 3, slot] = 1
    pick = np.zeros((96, 128), np.float32)
    for s in range(3):
        for r in range(13):
            row = r - 3
            start = UP + 8 * r if row < 0 else (DN + 8 * (row - 7) if row > 6 else 8 * row)
            pick[HIGH * s + r, start + s] = 1
            pick[48 + HIGH * s + r, start + 4 + s] = 1
    return key_row, key_col, perm, pick


KEY_ROW, KEY_COL, PERM, PICK = tables()


def nn(a, b):
    return lax.dot_general(a, b, (((1,), (0,)), ((), ())), preferred_element_type=F32)


def nt(a, b):
    return lax.dot_general(a, b, (((1,), (1,)), ((), ())), preferred_element_type=F32)


def tn(a, b):
    return lax.dot_general(a, b, (((0,), (0,)), ((), ())), preferred_element_type=F32)


def three_parts(x):
    high = x.astype(BF)
    rest = x - high.astype(F32)
    mid = rest.astype(BF)
    low = (rest - mid.astype(F32)).astype(BF)
    return high, mid, low


def front_kernel(s_ref, x_hbm, og_hbm, gain_hbm, wqkv_hbm, wproj_hbm, q_ref, kv_ref, ag_ref, m1_hbm, nb_ref, ogk_ref, nx_ref, inv_ref, a_ref, b_ref, xs, os, x_ref, og_ref, gain_ref, wqkv_ref, wproj_ref, m1_ref, sems):
    loads = [
        pltpu.make_async_copy(source, target, sems.at[i])
        for i, (source, target) in enumerate(((x_hbm, x_ref), (og_hbm, og_ref), (wqkv_hbm, wqkv_ref), (wproj_hbm, wproj_ref), (gain_hbm, gain_ref)))
    ]
    for load in loads:
        load.start()
    xs[...] = jnp.zeros_like(xs)
    os[...] = jnp.zeros_like(os)
    loads[0].wait()
    for t in range(3):
        for r in range(7):
            xs[t * 64 + r * 8 : t * 64 + r * 8 + 7, :] = x_ref[t, r].astype(F32)
    xf = xs[...]
    dev = xf - jnp.mean(xf, axis=-1, keepdims=True)
    inv = lax.rsqrt(jnp.mean(dev * dev, axis=-1, keepdims=True) + EPS)
    nx = dev * inv
    loads[4].wait()
    nx_ref[...] = nx
    inv_ref[...] = jnp.broadcast_to(inv, inv_ref.shape)
    normed = (nx * gain_ref[...]).astype(BF)
    nb_ref[...] = normed
    m1_ref[:, :1024] = normed
    sends = [pltpu.make_async_copy(m1_ref.at[:, lanes], m1_hbm.at[:, lanes], sems.at[5 + i]) for i, lanes in enumerate((slice(0, 1024), slice(1024, 1536)))]
    sends[0].start()
    loads[2].wait()
    qkv = nn(normed, wqkv_ref[...]).astype(BF)
    for t in range(3):
        rows = qkv[t * 64 : t * 64 + 64]
        q_ref[t] = rows[:, :512]
        kv_ref[t] = rows[:, 512:]

    @pl.when(s_ref[5] == 0)
    def _():
        for t in range(3):
            a_ref[t] = kv_ref[t, 32:56]
            b_ref[t] = kv_ref[t, 0:24]

    @pl.when(s_ref[5] != 0)
    def _():
        for t in range(3):
            a_ref[t] = kv_ref[t, 0:24]
            b_ref[t] = kv_ref[t, 32:56]

    loads[1].wait()
    for t in range(3):
        for r in range(7):
            os[t * 64 + r * 8 : t * 64 + r * 8 + 7, :] = og_ref[t, r].astype(F32)
    og = os[...].astype(BF)
    loads[3].wait()

    @pl.when(s_ref[0] == 0)
    def _():
        ogk_ref[...] = og[:, :512]
        m1_ref[:, 1024:] = og[:, 512:]

    @pl.when(s_ref[0] != 0)
    def _():
        ogk_ref[...] = og[:, 512:]
        m1_ref[:, 1024:] = og[:, :512]

    sends[1].start()
    ag_ref[...] = nt(og, wproj_ref[...]).astype(BF).reshape(3, 64, 512)
    sends[0].wait()
    sends[1].wait()


def columns_kernel(s_ref, kv_ref, got_a, got_b, pick_ref, edge_ref, a_ref, b_ref, rows):
    edge_ref[...] = jnp.zeros_like(edge_ref)

    @pl.when(s_ref[5] == 0)
    def _():
        for t in range(3):
            edge_ref[t, 0:24] = got_b[t]
            edge_ref[t, 32:56] = got_a[t]

    @pl.when(s_ref[5] != 0)
    def _():
        for t in range(3):
            edge_ref[t, 0:24] = got_a[t]
            edge_ref[t, 32:56] = got_b[t]

    for t in range(3):
        rows[t, 0:64] = kv_ref[t]
        rows[t, 64:128] = edge_ref[t]
    outs = [nn(pick_ref[...], rows[t]).astype(BF) for t in range(3)]

    @pl.when(s_ref[0] == 0)
    def _():
        for t in range(3):
            a_ref[t] = outs[t][48:88]
            b_ref[t] = outs[t][0:40]

    @pl.when(s_ref[0] != 0)
    def _():
        for t in range(3):
            a_ref[t] = outs[t][0:40]
            b_ref[t] = outs[t][48:88]


def table_kernel(s_ref, rel_ref, key_row_ref, key_col_ref, perm_ref, out_ref, grid_ref):
    grid_ref[...] = jnp.zeros_like(grid_ref)
    line = rel_ref[...]
    for r in range(7):
        for c in range(7):
            turned = pltpu.roll(line, ((r - 3) * 16 + c - 3) % 256, 1)
            for half in range(2):
                grid_ref.at[half][pl.ds(r * 8 + c, 8, stride=64), :] = turned[:, half * 128 : half * 128 + 128]
    high, mid, low = three_parts(jnp.concatenate([grid_ref[0], grid_ref[1]], axis=1))
    perm = perm_ref[...]
    table = nn(high, perm) + (nn(mid, perm) + nn(low, perm))
    place = lax.broadcasted_iota(jnp.int32, (64, 256), 0)
    row = place // 8
    col = place % 8
    row_first = jnp.clip(s_ref[1] + row - 3, 0, s_ref[3] - WIN) - s_ref[1]
    col_first = jnp.clip(s_ref[2] + col - 3, 0, s_ref[4] - WIN) - s_ref[2]
    key_row = key_row_ref[...]
    key_col = key_col_ref[...]
    valid = (key_row >= row_first) & (key_row < row_first + WIN) & (key_col >= col_first) & (key_col < col_first + WIN) & (row < 7) & (col < 7)
    for h in range(8):
        out_ref[h * 64 : h * 64 + 64, :] = jnp.where(valid, table[h * 64 : h * 64 + 64], -1e30)


def attention_kernel(s_ref, q_ref, kv_ref, edge_ref, got_a, got_b, ag_ref, table_ref, att_ref, dq_ref, own_ref, a_ref, b_ref, g_ref, keys, dkv):
    keys[:, 160:256, :] = jnp.zeros((3, 96, 1024), BF)
    for t in range(3):
        keys[t, 0:64] = kv_ref[t]
        keys[t, 64:128] = edge_ref[t]

    @pl.when(s_ref[0] == 0)
    def _():
        for t in range(3):
            keys[t, LF : LF + 40] = got_b[t]
            keys[t, RT : RT + 40] = got_a[t]

    @pl.when(s_ref[0] != 0)
    def _():
        for t in range(3):
            keys[t, LF : LF + 40] = got_a[t]
            keys[t, RT : RT + 40] = got_b[t]

    at_row = lax.broadcasted_iota(jnp.int32, (256, 256), 0) // 64
    at_col = lax.broadcasted_iota(jnp.int32, (256, 256), 1) // 64
    diag = at_row == at_col

    def spread(x):
        x = x.astype(F32)
        return jnp.where(diag, jnp.concatenate([x, x, x, x], axis=0), 0.0).astype(BF)

    def gather(x):
        x = jnp.where(diag, x, 0.0)
        return (x[0:64] + x[64:128]) + (x[128:192] + x[192:256])

    totals = [None, None]
    for t in range(3):
        for g in range(2):
            at = slice(g * 256, g * 256 + 256)
            k = keys[t, :, g * 256 : g * 256 + 256]
            v = keys[t, :, 512 + g * 256 : 768 + g * 256]
            qb = spread(q_ref[t, :, at])
            db = spread(ag_ref[t, :, at])
            scores = nt(qb, k) * 0.125 + table_ref[at, :]
            terms = jnp.exp(scores - jnp.max(scores, axis=-1, keepdims=True))
            probs = terms / jnp.sum(terms, axis=-1, keepdims=True)
            low = probs.astype(BF)
            att_ref[t, :, at] = gather(nn(low, v)).astype(BF)
            dprobs = nt(db, v)
            dscores = probs * (dprobs - jnp.sum(probs * dprobs, axis=-1, keepdims=True))
            totals[g] = dscores if t == 0 else totals[g] + dscores
            dlow = dscores.astype(BF)
            dq_ref[t, :, at] = (gather(nn(dlow, k)) * 0.125).astype(BF)
            for lanes, grad in ((at, tn(dlow, qb) * 0.125), (slice(512 + g * 256, 768 + g * 256), tn(low, db))):
                own_ref[t, :, lanes] = grad[0:128]
                dkv[t, :, lanes] = grad[128:224].astype(BF)

    @pl.when(s_ref[0] == 0)
    def _():
        for t in range(3):
            a_ref[t] = dkv[t, 48:88]
            b_ref[t] = dkv[t, 0:40]

    @pl.when(s_ref[0] != 0)
    def _():
        for t in range(3):
            a_ref[t] = dkv[t, 0:40]
            b_ref[t] = dkv[t, 48:88]

    g_ref[0:256] = totals[0]
    g_ref[256:512] = totals[1]


def out_kernel(att_ref, wproj_ref, x_ref, g_ref, perm_ref, out_ref, bias_ref, ys, gs):
    ys[...] = nn(att_ref[...].reshape(192, 512), wproj_ref[...])
    for t in range(3):
        for r in range(7):
            out_ref[t, r] = (x_ref[t, r].astype(F32) + ys[t * 64 + r * 8 : t * 64 + r * 8 + 7, :]).astype(BF)
    high, mid, low = three_parts(g_ref[...])
    perm = perm_ref[...]
    grid = nt(high, perm) + (nt(mid, perm) + nt(low, perm))
    for half in range(2):
        gs[half] = grid[:, half * 128 : half * 128 + 128]
    total = None
    for r in range(7):
        for c in range(7):
            part = jnp.concatenate([gs.at[half][pl.ds(r * 8 + c, 8, stride=64), :] for half in range(2)], axis=1)
            part = pltpu.roll(part, ((3 - r) * 16 + 3 - c) % 256, 1)
            total = part if total is None else total + part
    bias_ref[...] = total


def edges_kernel(s_ref, own_ref, pick_ref, got_a, got_b, bias_ref, sum_ref, a_ref, b_ref, side):
    side[...] = jnp.zeros_like(side)

    @pl.when(s_ref[0] == 0)
    def _():
        for t in range(3):
            side[t, 0:40] = got_b[t]
            side[t, 48:88] = got_a[t]

    @pl.when(s_ref[0] != 0)
    def _():
        for t in range(3):
            side[t, 0:40] = got_a[t]
            side[t, 48:88] = got_b[t]

    totals = [own_ref[t] + tn(pick_ref[...], side[t]) for t in range(3)]
    for t in range(3):
        sum_ref[t] = totals[t][0:64]

    @pl.when(s_ref[5] == 0)
    def _():
        for t in range(3):
            a_ref[t] = totals[t][96:120].astype(BF)
            b_ref[t] = totals[t][64:88].astype(BF)

    @pl.when(s_ref[5] != 0)
    def _():
        for t in range(3):
            a_ref[t] = totals[t][64:88].astype(BF)
            b_ref[t] = totals[t][96:120].astype(BF)


def join_kernel(s_ref, sum_ref, dq_ref, att_ref, got_a, got_b, bias_ref, dqkv_ref, m2_ref, acc):
    acc[...] = sum_ref[...]

    @pl.when(s_ref[5] == 0)
    def _():
        for t in range(3):
            acc[t, 32:56] = acc[t, 32:56] + got_a[t].astype(F32)
            acc[t, 0:24] = acc[t, 0:24] + got_b[t].astype(F32)

    @pl.when(s_ref[5] != 0)
    def _():
        for t in range(3):
            acc[t, 0:24] = acc[t, 0:24] + got_a[t].astype(F32)
            acc[t, 32:56] = acc[t, 32:56] + got_b[t].astype(F32)

    for t in range(3):
        dqkv_ref[t * 64 : t * 64 + 64, 0:512] = dq_ref[t]
        dqkv_ref[t * 64 : t * 64 + 64, 512:1536] = acc[t].astype(BF)
    m2_ref[:, 0:512] = att_ref[...].reshape(192, 512)

    @pl.when(s_ref[0] == 0)
    def _():
        m2_ref[:, 512:1280] = dqkv_ref[:, 768:1536]

    @pl.when(s_ref[0] != 0)
    def _():
        m2_ref[:, 512:1280] = dqkv_ref[:, 0:768]


def feats_kernel(dqkv_ref, wqkv_ref, nx_ref, inv_ref, gain_ref, og_ref, out_ref, gg_ref, ys):
    ngrad = nt(dqkv_ref[...], wqkv_ref[...])
    nx = nx_ref[...]
    gg_ref[...] = jnp.sum(ngrad * nx, axis=0, keepdims=True)
    scaled = ngrad * gain_ref[...]
    correction = scaled - jnp.mean(scaled, axis=-1, keepdims=True) - nx * jnp.mean(scaled * nx, axis=-1, keepdims=True)
    ys[...] = inv_ref[:, 0:1] * correction
    for t in range(3):
        for r in range(7):
            out_ref[t, r] = (og_ref[t, r].astype(F32) + ys[t * 64 + r * 8 : t * 64 + r * 8 + 7, :]).astype(BF)


def put_small(write, bias, gain_rows):
    high = bias.astype(BF)
    write(slice(0, 256), high)
    write(slice(256, 512), (bias - high.astype(F32)).astype(BF))
    high = gain_rows.astype(BF)
    write(slice(512, 640), high)
    write(slice(640, 768), (gain_rows - high.astype(F32)).astype(BF))
    write(slice(768, 1024), jnp.zeros((8, 256), BF))


def get_small(block):
    return block[:, 0:256] + block[:, 256:512], block[:, 512:640] + block[:, 640:768]


def weights_kernel(s_ref, nb_ref, att_ref, dqkv_ref, ogk_ref, m1_ref, m2_ref, gg_ref, bias_ref, out_ref, zq, zp, gs):
    count = out_ref.shape[0]
    tall = 1024 // count

    @pl.when(s_ref[0] == 0)
    def _():
        zq[...] = tn(nb_ref[...], dqkv_ref[:, 0:768]) + tn(m1_ref[:, 0:1024], m2_ref[:, 512:1280])

    @pl.when(s_ref[0] != 0)
    def _():
        zq[...] = tn(nb_ref[...], dqkv_ref[:, 768:1536]) + tn(m1_ref[:, 0:1024], m2_ref[:, 512:1280])

    zp[...] = tn(att_ref[...].reshape(192, 512), ogk_ref[...]) + tn(m2_ref[:, 0:512], m1_ref[:, 1024:1536])
    for j in range(8):
        gs[j : j + 1, :] = gg_ref[:, j * 128 : j * 128 + 128]
    for i in range(count):
        out_ref[i, 0:tall, 0:768] = zq[i * tall : i * tall + tall].astype(BF)
        first = i * tall
        out_ref[i, 0:tall, 768:1024] = zp[first % 512 : first % 512 + tall, first // 512 * 256 : first // 512 * 256 + 256].astype(BF)

        def write(lanes, value, i=i):
            out_ref[i, tall : tall + 8, lanes] = value

        put_small(write, bias_ref[...], gs[...])


def axis_sum_kernel(y_ref, out_ref):
    count = y_ref.shape[0]
    total = y_ref[0].astype(F32)
    for i in range(1, count):
        total = total + y_ref[i].astype(F32)
    groups = out_ref.shape[0]
    tall = out_ref.shape[1] - 8
    bias, gain_rows = get_small(total[groups * tall : groups * tall + 8])
    for j in range(groups):
        out_ref[j, 0:tall] = total[j * tall : j * tall + tall].astype(BF)

        def write(lanes, value, j=j):
            out_ref[j, tall : tall + 8, lanes] = value

        put_small(write, bias, gain_rows)


def first_sum_kernel(y_ref, out_ref):
    count = y_ref.shape[0]
    total = y_ref[0].astype(F32)
    for i in range(1, count):
        total = total + y_ref[i].astype(F32)
    groups, tall = out_ref.shape[:2]
    bias, gain_rows = get_small(total[groups * tall : groups * tall + 8])
    small = jnp.concatenate([bias[:, 0:128], bias[:, 128:256], gain_rows, jnp.zeros((8, 128), F32)], axis=0)
    share = 32 // groups
    zeros = jnp.zeros((tall - 2 * share, 128), F32) if tall > 2 * share else None
    for j in range(groups):
        out_ref[j, :, 0:1024] = total[j * tall : j * tall + tall].astype(BF)
        part = small[j * share : j * share + share]
        high = part.astype(BF).astype(F32)
        pieces = [high, part - high] + ([] if zeros is None else [zeros])
        out_ref[j, :, 1024:1152] = jnp.concatenate(pieces, axis=0).astype(BF)


def second_sum_kernel(y_ref, out_ref):
    count = y_ref.shape[0]
    total = y_ref[0].astype(F32)
    for i in range(1, count):
        total = total + y_ref[i].astype(F32)
    groups, tall = out_ref.shape[:2]
    share = 32 // groups
    main = total[:, 0:1024].astype(BF)
    part = total[0:share, 1024:1152] + total[share : 2 * share, 1024:1152]
    high = part.astype(BF).astype(F32)
    pieces = [high, part - high] + ([jnp.zeros((tall - 2 * share, 128), F32)] if tall > 2 * share else [])
    side = jnp.concatenate(pieces, axis=0).astype(BF)
    for j in range(groups):
        out_ref[j, :, 0:1024] = main
        out_ref[j, :, 1024:1152] = side


def spread_kernel(y_ref, out_ref, small_ref):
    groups, tall = y_ref.shape[:2]
    small_ref[...] = y_ref[:, :, 1024:1152]
    for j in range(groups):
        part = y_ref[j, :, 0:1024]
        for i in range(out_ref.shape[0]):
            out_ref[i, j * tall : j * tall + tall] = part


def small_kernel(small_ref, other_ref, out_ref):
    groups = small_ref.shape[0]
    share = 32 // groups
    for j in range(groups):
        both = small_ref[j].astype(F32) + other_ref[j].astype(F32)
        out_ref[j * share : j * share + share, :] = both[0:share] + both[share : 2 * share]


def place(c, ref, qkv_ref, proj_ref, sems):
    copies = [pltpu.make_async_copy(ref.at[:, 0:768], qkv_ref.at[:, c * 768 : c * 768 + 768], sems.at[0])]
    for j in range(2):
        copies.append(pltpu.make_async_copy(ref.at[j * 512 : j * 512 + 512, 768:1024], proj_ref.at[:, c * 512 + j * 256 : c * 512 + j * 256 + 256], sems.at[1 + j]))
    for copy in copies:
        copy.start()
    for copy in copies:
        copy.wait()


def mine_kernel(s_ref, mine_ref, qkv_ref, proj_ref, sems):
    @pl.when(s_ref[0] == 0)
    def _():
        place(0, mine_ref, qkv_ref, proj_ref, sems)

    @pl.when(s_ref[0] != 0)
    def _():
        place(1, mine_ref, qkv_ref, proj_ref, sems)


def theirs_kernel(s_ref, theirs_ref, qkv_in, proj_in, qkv_ref, proj_ref, sems):
    @pl.when(s_ref[0] == 0)
    def _():
        place(1, theirs_ref, qkv_ref, proj_ref, sems)

    @pl.when(s_ref[0] != 0)
    def _():
        place(0, theirs_ref, qkv_ref, proj_ref, sems)


def call(kernel, outs, args, scratch=(), name=None, left=(), sems=0, outs_left=(), aliases=None, grant=24, pinned=()):
    def spec(i, a):
        space = pltpu.SMEM if a.dtype == jnp.int32 and a.ndim == 1 else pltpu.HBM if i in left else pltpu.VMEM
        return pl.BlockSpec(memory_space=space)

    specs = [spec(i, a) for i, a in enumerate(args)]
    args = [pltpu.with_memory_space_constraint(a, pltpu.HBM) if i in left and not INTERPRET else a for i, a in enumerate(args)]
    return pl.pallas_call(
        kernel,
        out_shape=[pltpu.HBM(shape, kind) if (i in pinned or i in outs_left) and not INTERPRET else jax.ShapeDtypeStruct(shape, kind) for i, (shape, kind) in enumerate(outs)],
        in_specs=specs,
        out_specs=[pl.BlockSpec(memory_space=pltpu.HBM if i in outs_left else pltpu.VMEM) for i in range(len(outs))],
        input_output_aliases=aliases or {},
        scratch_shapes=[pltpu.VMEM(shape, kind) for shape, kind in scratch] + ([pltpu.SemaphoreType.DMA((sems,))] if sems else []),
        compiler_params=pltpu.CompilerParams(vmem_limit_bytes=grant * 1024 * 1024),
        interpret=INTERPRET,
        name=name,
    )(*args)


def make_body(sizes):
    zl, nx_, zh, ny, nc = sizes
    rows, cols = zl * nx_, zh * ny * nc
    every = ("zl", "x", "zh", "y", "c")
    deep = zl * zh
    ids = np.arange(rows * cols).reshape(sizes)
    along_x = [[[int(v) for v in ids[a, :, b, k, c]] for a in range(zl) for b in range(zh) for k in range(ny)] for c in range(nc)]
    along_y = [[[int(v) for v in ids[a, k, b, :, c]] for a in range(zl) for b in range(zh) for k in range(nx_)] for c in range(nc)]
    first_groups = along_x[0] + along_y[1]
    second_groups = along_y[0] + along_x[1]
    assert nx_ == ny and nc == 2

    def row_pairs(value, first):
        pairs = []
        for low in range(first, rows - 1, 2):
            for j in range(cols):
                pairs += [(low * cols + j, (low + 1) * cols + j), ((low + 1) * cols + j, low * cols + j)]
        return lax.ppermute(value, every, pairs)

    def col_pairs(value, first):
        pairs = []
        for low in range(first, cols - 1, 2):
            for i in range(rows):
                pairs += [(i * cols + low, i * cols + low + 1), (i * cols + low + 1, i * cols + low)]
        return lax.ppermute(value, every, pairs)

    def trade(value, groups):
        return lax.all_to_all(value, every, 0, 0, tiled=True, axis_index_groups=groups)

    def trade_deep(value):
        return lax.all_to_all(value, ("zl", "zh"), 0, 0, tiled=True)

    def swap(value):
        return lax.ppermute(value, "c", [(0, 1), (1, 0)])

    def body(image_feats, norm_gain, w_qkv, rel_bias, w_proj, out_grad):
        core = lax.axis_index("c")
        row_anchor = (lax.axis_index("zl") * nx_ + lax.axis_index("x")) * 7
        col_anchor = ((lax.axis_index("zh") * ny + lax.axis_index("y")) * nc + core) * 7
        scalars = jnp.stack([core, row_anchor, col_anchor, jnp.int32(rows * 7), jnp.int32(cols * 7), (row_anchor // 7) % 2]).astype(jnp.int32)
        gain = norm_gain.reshape(1, 1024)
        pick = jnp.asarray(PICK, BF)
        perm = jnp.asarray(PERM, BF)
        rel = jnp.pad(rel_bias, ((0, 0), (0, 3), (0, 3))).reshape(8, 256)
        queries, own_kv, attn_grad, m1, normed, og_keep, normal_x, inv_std, row_a, row_b = call(
            front_kernel,
            [((3, 64, 512), BF), ((3, 64, 1024), BF), ((3, 64, 512), BF), ((192, 1536), BF), ((192, 1024), BF), ((192, 512), BF), ((192, 1024), F32), ((192, 128), F32), ((3, 24, 1024), BF), ((3, 24, 1024), BF)],
            [scalars, image_feats, out_grad, gain, w_qkv, w_proj],
            [((192, 1024), F32), ((192, 1024), F32), ((3, 7, 7, 1024), BF), ((3, 7, 7, 1024), BF), ((1, 1024), F32), ((1024, 1536), BF), ((512, 1024), BF), ((192, 1536), BF)],
            "front",
            (1, 2, 3, 4, 5),
            7,
            (3,),
            pinned=(4, 5, 6, 7),
        )
        row_b = row_pairs(row_b, 1)
        row_a = row_pairs(row_a, 0)
        (table,) = call(
            table_kernel,
            [((512, 256), F32)],
            [scalars, rel, jnp.asarray(KEY_ROW), jnp.asarray(KEY_COL), perm],
            [((2, 512, 128), F32)],
            "table",
        )
        edges, col_a, col_b = call(
            columns_kernel,
            [((3, 64, 1024), BF), ((3, 40, 1024), BF), ((3, 40, 1024), BF)],
            [scalars, own_kv, row_a, row_b, pick],
            [((3, 128, 1024), BF)],
            "columns",
        )
        col_b = col_pairs(col_b, 1)
        col_a = col_pairs(col_a, 0)
        attended, query_grad, own_grad, col_a, col_b, score_sum = call(
            attention_kernel,
            [((3, 64, 512), BF), ((3, 64, 512), BF), ((3, 128, 1024), F32), ((3, 40, 1024), BF), ((3, 40, 1024), BF), ((512, 256), F32)],
            [scalars, queries, own_kv, edges, col_a, col_b, attn_grad, table],
            [((3, 256, 1024), BF), ((3, 96, 1024), BF)],
            "attention",
        )
        col_b = col_pairs(col_b, 1)
        col_a = col_pairs(col_a, 0)
        m1_other = swap(m1)
        layer_out, bias_part = call(
            out_kernel,
            [((3, 7, 7, 1024), BF), ((8, 256), F32)],
            [attended, w_proj, image_feats, score_sum, perm],
            [((192, 1024), F32), ((2, 512, 128), F32)],
            "layer_out",
        )
        own_sum, row_a, row_b = call(
            edges_kernel,
            [((3, 64, 1024), F32), ((3, 24, 1024), BF), ((3, 24, 1024), BF)],
            [scalars, own_grad, pick, col_a, col_b, bias_part],
            [((3, 96, 1024), BF)],
            "edges",
        )
        row_b = row_pairs(row_b, 1)
        row_a = row_pairs(row_a, 0)
        dqkv, m2 = call(
            join_kernel,
            [((192, 1536), BF), ((192, 1280), BF)],
            [scalars, own_sum, query_grad, attended, row_a, row_b, bias_part],
            [((3, 64, 1024), F32)],
            "join",
        )
        m2_other = swap(m2)
        feats_grad, gain_part = call(
            feats_kernel,
            [((3, 7, 7, 1024), BF), ((1, 1024), F32)],
            [dqkv, w_qkv, normal_x, inv_std, gain, out_grad],
            [((192, 1024), F32)],
            "feats",
        )
        tall1 = 1024 // nx_
        tall2 = tall1 // ny
        tall3 = tall2 // deep
        (send,) = call(
            weights_kernel,
            [((nx_, tall1 + 8, 1024), BF)],
            [scalars, normed, attended, dqkv, og_keep, m1_other, m2_other, gain_part, bias_part],
            [((1024, 768), F32), ((512, 512), F32), ((8, 128), F32)],
            "weights",
        )
        send = trade(send, first_groups)
        (send,) = call(axis_sum_kernel, [((ny, tall2 + 8, 1024), BF)], [send], (), "first_sum")
        send = trade(send, second_groups)
        (send,) = call(first_sum_kernel, [((deep, tall3, 1152), BF)], [send], (), "second_sum")
        send = trade_deep(send)
        (send,) = call(second_sum_kernel, [((deep, tall3, 1152), BF)], [send], (), "third_sum")
        send = trade_deep(send)
        send, small = call(spread_kernel, [((ny, tall2, 1024), BF), ((deep, tall3, 128), BF)], [send], (), "spread")
        small_other = swap(small)
        send = trade(send, second_groups).reshape(1, tall1, 1024)
        send, small_other = lax.optimization_barrier((send, small_other))
        mine = trade(jnp.broadcast_to(send, (nx_, tall1, 1024)), first_groups).reshape(1024, 1024)
        theirs = swap(mine)
        weight_outs = [((1024, 1536), BF), ((512, 1024), BF)]
        (small,) = call(small_kernel, [((32, 128), F32)], [small, small_other], (), "small")
        qkv_grad, proj_grad = call(mine_kernel, weight_outs, [scalars, mine], (), "mine", (), 3, (0, 1))
        qkv_grad, proj_grad = call(theirs_kernel, weight_outs, [scalars, theirs, qkv_grad, proj_grad], (), "theirs", (2, 3), 3, (0, 1), {2: 0, 3: 1})
        gain_grad = small[16:24].reshape(1024)
        bias_grad = jnp.concatenate([small[0:8], small[8:16]], axis=1).reshape(8, 16, 16)[:, :13, :13]
        return (layer_out, feats_grad, qkv_grad, proj_grad, gain_grad, bias_grad)

    return body


def solution(mesh, sizes=(2, 4, 4, 4, 2)):
    fine = Mesh(mesh.devices.reshape(sizes), ("zl", "x", "zh", "y", "c"))
    image = P(None, ("zl", "x"), ("zh", "y", "c"), None)
    return jax.shard_map(
        make_body(sizes),
        mesh=fine,
        in_specs=(image, P(), P(), P(), P(), image),
        out_specs=(image, image, P(), P(), P(), P()),
        check_vma=False,
    )
```

```python
import numpy as np
import jax
import jax.numpy as jnp
from jax import lax
from jax.experimental import pallas as pl
from jax.experimental.pallas import tpu as pltpu
from jax.sharding import Mesh
from jax.sharding import PartitionSpec as P

WIN = 7
EPS = 1e-05
BF = jnp.bfloat16
F32 = jnp.float32
INTERPRET = False

UP, DN, LF, RT = 64, 96, 128, 176
HIGH = 13


def tables():
    key_row = np.full((1, 256), -100, np.int32)
    key_col = np.full((1, 256), -100, np.int32)
    for r in range(7):
        for c in range(7):
            key_row[0, 8 * r + c] = r
            key_col[0, 8 * r + c] = c
    for s in range(3):
        for c in range(7):
            for slot, row in ((UP, s - 3), (DN, 7 + s)):
                key_row[0, slot + 8 * s + c] = row
                key_col[0, slot + 8 * s + c] = c
        for r in range(13):
            for slot, col in ((LF, s - 3), (RT, 7 + s)):
                key_row[0, slot + HIGH * s + r] = r - 3
                key_col[0, slot + HIGH * s + r] = col
    perm = np.zeros((256, 256), np.float32)
    for slot in range(256):
        if key_row[0, slot] > -100:
            perm[(key_row[0, slot] + 3) * 16 + key_col[0, slot] + 3, slot] = 1
    pick = np.zeros((96, 128), np.float32)
    for s in range(3):
        for r in range(13):
            row = r - 3
            start = UP + 8 * r if row < 0 else (DN + 8 * (row - 7) if row > 6 else 8 * row)
            pick[HIGH * s + r, start + s] = 1
            pick[48 + HIGH * s + r, start + 4 + s] = 1
    return key_row, key_col, perm, pick


KEY_ROW, KEY_COL, PERM, PICK = tables()


def nn(a, b):
    return lax.dot_general(a, b, (((1,), (0,)), ((), ())), preferred_element_type=F32)


def nt(a, b):
    return lax.dot_general(a, b, (((1,), (1,)), ((), ())), preferred_element_type=F32)


def tn(a, b):
    return lax.dot_general(a, b, (((0,), (0,)), ((), ())), preferred_element_type=F32)


def three_parts(x):
    high = x.astype(BF)
    rest = x - high.astype(F32)
    mid = rest.astype(BF)
    low = (rest - mid.astype(F32)).astype(BF)
    return high, mid, low


def front_kernel(s_ref, x_hbm, og_hbm, gain_hbm, wqkv_hbm, wproj_hbm, q_ref, kv_ref, ag_ref, m1_hbm, ogk_ref, nx_hbm, inv_ref, a_ref, b_ref, xs, os, x_ref, og_ref, gain_ref, wqkv_ref, wproj_ref, m1_ref, nx_ref, sems):
    loads = [
        pltpu.make_async_copy(source, target, sems.at[i])
        for i, (source, target) in enumerate(((x_hbm, x_ref), (og_hbm, og_ref), (wqkv_hbm, wqkv_ref), (wproj_hbm, wproj_ref), (gain_hbm, gain_ref)))
    ]
    for load in loads:
        load.start()
    xs[...] = jnp.zeros_like(xs)
    os[...] = jnp.zeros_like(os)
    loads[0].wait()
    for t in range(3):
        for r in range(7):
            xs[t * 64 + r * 8 : t * 64 + r * 8 + 7, :] = x_ref[t, r].astype(F32)
    xf = xs[...]
    dev = xf - jnp.mean(xf, axis=-1, keepdims=True)
    inv = lax.rsqrt(jnp.mean(dev * dev, axis=-1, keepdims=True) + EPS)
    nx = dev * inv
    loads[4].wait()
    nx_ref[...] = nx
    inv_ref[...] = jnp.broadcast_to(inv, inv_ref.shape)
    normed = (nx * gain_ref[...]).astype(BF)
    m1_ref[:, :1024] = normed
    sends = [pltpu.make_async_copy(m1_ref.at[:, lanes], m1_hbm.at[:, lanes], sems.at[5 + i]) for i, lanes in enumerate((slice(0, 1024), slice(1024, 1536)))]
    sends.append(pltpu.make_async_copy(nx_ref, nx_hbm, sems.at[7]))
    sends[0].start()
    sends[2].start()
    loads[2].wait()
    qkv = nn(normed, wqkv_ref[...]).astype(BF)
    for t in range(3):
        rows = qkv[t * 64 : t * 64 + 64]
        q_ref[t] = rows[:, :512]
        kv_ref[t] = rows[:, 512:]

    @pl.when(s_ref[5] == 0)
    def _():
        for t in range(3):
            a_ref[t] = kv_ref[t, 32:56]
            b_ref[t] = kv_ref[t, 0:24]

    @pl.when(s_ref[5] != 0)
    def _():
        for t in range(3):
            a_ref[t] = kv_ref[t, 0:24]
            b_ref[t] = kv_ref[t, 32:56]

    loads[1].wait()
    for t in range(3):
        for r in range(7):
            os[t * 64 + r * 8 : t * 64 + r * 8 + 7, :] = og_ref[t, r].astype(F32)
    og = os[...].astype(BF)
    loads[3].wait()

    @pl.when(s_ref[0] == 0)
    def _():
        ogk_ref[...] = og[:, :512]
        m1_ref[:, 1024:] = og[:, 512:]

    @pl.when(s_ref[0] != 0)
    def _():
        ogk_ref[...] = og[:, 512:]
        m1_ref[:, 1024:] = og[:, :512]

    sends[1].start()
    ag_ref[...] = nt(og, wproj_ref[...]).astype(BF).reshape(3, 64, 512)
    for send in sends:
        send.wait()


def columns_kernel(s_ref, kv_ref, got_a, got_b, pick_ref, edge_ref, a_ref, b_ref, rows):
    edge_ref[...] = jnp.zeros_like(edge_ref)

    @pl.when(s_ref[5] == 0)
    def _():
        for t in range(3):
            edge_ref[t, 0:24] = got_b[t]
            edge_ref[t, 32:56] = got_a[t]

    @pl.when(s_ref[5] != 0)
    def _():
        for t in range(3):
            edge_ref[t, 0:24] = got_a[t]
            edge_ref[t, 32:56] = got_b[t]

    for t in range(3):
        rows[t, 0:64] = kv_ref[t]
        rows[t, 64:128] = edge_ref[t]
    outs = [nn(pick_ref[...], rows[t]).astype(BF) for t in range(3)]

    @pl.when(s_ref[0] == 0)
    def _():
        for t in range(3):
            a_ref[t] = outs[t][48:88]
            b_ref[t] = outs[t][0:40]

    @pl.when(s_ref[0] != 0)
    def _():
        for t in range(3):
            a_ref[t] = outs[t][0:40]
            b_ref[t] = outs[t][48:88]


def table_kernel(s_ref, rel_ref, key_row_ref, key_col_ref, perm_ref, out_ref, grid_ref):
    grid_ref[...] = jnp.zeros_like(grid_ref)
    line = rel_ref[...]
    for r in range(7):
        for c in range(7):
            turned = pltpu.roll(line, ((r - 3) * 16 + c - 3) % 256, 1)
            for half in range(2):
                grid_ref.at[half][pl.ds(r * 8 + c, 8, stride=64), :] = turned[:, half * 128 : half * 128 + 128]
    high, mid, low = three_parts(jnp.concatenate([grid_ref[0], grid_ref[1]], axis=1))
    perm = perm_ref[...]
    table = nn(high, perm) + (nn(mid, perm) + nn(low, perm))
    place = lax.broadcasted_iota(jnp.int32, (64, 256), 0)
    row = place // 8
    col = place % 8
    row_first = jnp.clip(s_ref[1] + row - 3, 0, s_ref[3] - WIN) - s_ref[1]
    col_first = jnp.clip(s_ref[2] + col - 3, 0, s_ref[4] - WIN) - s_ref[2]
    key_row = key_row_ref[...]
    key_col = key_col_ref[...]
    valid = (key_row >= row_first) & (key_row < row_first + WIN) & (key_col >= col_first) & (key_col < col_first + WIN) & (row < 7) & (col < 7)
    for h in range(8):
        out_ref[h * 64 : h * 64 + 64, :] = jnp.where(valid, table[h * 64 : h * 64 + 64], -1e30)


def attention_kernel(s_ref, q_ref, kv_ref, edge_ref, got_a, got_b, ag_ref, table_ref, att_ref, dq_ref, own_ref, a_ref, b_ref, g_ref, keys, dkv):
    keys[:, 160:256, :] = jnp.zeros((3, 96, 1024), BF)
    for t in range(3):
        keys[t, 0:64] = kv_ref[t]
        keys[t, 64:128] = edge_ref[t]

    @pl.when(s_ref[0] == 0)
    def _():
        for t in range(3):
            keys[t, LF : LF + 40] = got_b[t]
            keys[t, RT : RT + 40] = got_a[t]

    @pl.when(s_ref[0] != 0)
    def _():
        for t in range(3):
            keys[t, LF : LF + 40] = got_a[t]
            keys[t, RT : RT + 40] = got_b[t]

    at_row = lax.broadcasted_iota(jnp.int32, (256, 256), 0) // 64
    at_col = lax.broadcasted_iota(jnp.int32, (256, 256), 1) // 64
    diag = at_row == at_col

    def spread(x):
        x = x.astype(F32)
        return jnp.where(diag, jnp.concatenate([x, x, x, x], axis=0), 0.0).astype(BF)

    def gather(x):
        x = jnp.where(diag, x, 0.0)
        return (x[0:64] + x[64:128]) + (x[128:192] + x[192:256])

    totals = [None, None]
    for t in range(3):
        for g in range(2):
            at = slice(g * 256, g * 256 + 256)
            k = keys[t, :, g * 256 : g * 256 + 256]
            v = keys[t, :, 512 + g * 256 : 768 + g * 256]
            qb = spread(q_ref[t, :, at])
            db = spread(ag_ref[t, :, at])
            scores = nt(qb, k) * 0.125 + table_ref[at, :]
            terms = jnp.exp(scores - jnp.max(scores, axis=-1, keepdims=True))
            probs = terms / jnp.sum(terms, axis=-1, keepdims=True)
            low = probs.astype(BF)
            att_ref[t, :, at] = gather(nn(low, v)).astype(BF)
            dprobs = nt(db, v)
            dscores = probs * (dprobs - jnp.sum(probs * dprobs, axis=-1, keepdims=True))
            totals[g] = dscores if t == 0 else totals[g] + dscores
            dlow = dscores.astype(BF)
            dq_ref[t, :, at] = (gather(nn(dlow, k)) * 0.125).astype(BF)
            for lanes, grad in ((at, tn(dlow, qb) * 0.125), (slice(512 + g * 256, 768 + g * 256), tn(low, db))):
                own_ref[t, :, lanes] = grad[0:128]
                dkv[t, :, lanes] = grad[128:224].astype(BF)

    @pl.when(s_ref[0] == 0)
    def _():
        for t in range(3):
            a_ref[t] = dkv[t, 48:88]
            b_ref[t] = dkv[t, 0:40]

    @pl.when(s_ref[0] != 0)
    def _():
        for t in range(3):
            a_ref[t] = dkv[t, 0:40]
            b_ref[t] = dkv[t, 48:88]

    g_ref[0:256] = totals[0]
    g_ref[256:512] = totals[1]


def out_kernel(att_ref, wproj_ref, x_ref, g_ref, perm_ref, out_ref, bias_ref, ys, gs):
    ys[...] = nn(att_ref[...].reshape(192, 512), wproj_ref[...])
    for t in range(3):
        for r in range(7):
            out_ref[t, r] = (x_ref[t, r].astype(F32) + ys[t * 64 + r * 8 : t * 64 + r * 8 + 7, :]).astype(BF)
    high, mid, low = three_parts(g_ref[...])
    perm = perm_ref[...]
    grid = nt(high, perm) + (nt(mid, perm) + nt(low, perm))
    for half in range(2):
        gs[half] = grid[:, half * 128 : half * 128 + 128]
    total = None
    for r in range(7):
        for c in range(7):
            part = jnp.concatenate([gs.at[half][pl.ds(r * 8 + c, 8, stride=64), :] for half in range(2)], axis=1)
            part = pltpu.roll(part, ((3 - r) * 16 + 3 - c) % 256, 1)
            total = part if total is None else total + part
    bias_ref[...] = total


def edges_kernel(s_ref, own_ref, pick_ref, got_a, got_b, bias_ref, sum_ref, a_ref, b_ref, side):
    side[...] = jnp.zeros_like(side)

    @pl.when(s_ref[0] == 0)
    def _():
        for t in range(3):
            side[t, 0:40] = got_b[t]
            side[t, 48:88] = got_a[t]

    @pl.when(s_ref[0] != 0)
    def _():
        for t in range(3):
            side[t, 0:40] = got_a[t]
            side[t, 48:88] = got_b[t]

    totals = [own_ref[t] + tn(pick_ref[...], side[t]) for t in range(3)]
    for t in range(3):
        sum_ref[t] = totals[t][0:64]

    @pl.when(s_ref[5] == 0)
    def _():
        for t in range(3):
            a_ref[t] = totals[t][96:120].astype(BF)
            b_ref[t] = totals[t][64:88].astype(BF)

    @pl.when(s_ref[5] != 0)
    def _():
        for t in range(3):
            a_ref[t] = totals[t][64:88].astype(BF)
            b_ref[t] = totals[t][96:120].astype(BF)


def join_kernel(s_ref, sum_ref, dq_ref, att_ref, got_a, got_b, bias_ref, dqkv_ref, m2_ref, acc):
    acc[...] = sum_ref[...]

    @pl.when(s_ref[5] == 0)
    def _():
        for t in range(3):
            acc[t, 32:56] = acc[t, 32:56] + got_a[t].astype(F32)
            acc[t, 0:24] = acc[t, 0:24] + got_b[t].astype(F32)

    @pl.when(s_ref[5] != 0)
    def _():
        for t in range(3):
            acc[t, 0:24] = acc[t, 0:24] + got_a[t].astype(F32)
            acc[t, 32:56] = acc[t, 32:56] + got_b[t].astype(F32)

    for t in range(3):
        dqkv_ref[t * 64 : t * 64 + 64, 0:512] = dq_ref[t]
        dqkv_ref[t * 64 : t * 64 + 64, 512:1536] = acc[t].astype(BF)
    m2_ref[:, 0:512] = att_ref[...].reshape(192, 512)

    @pl.when(s_ref[0] == 0)
    def _():
        m2_ref[:, 512:1280] = dqkv_ref[:, 768:1536]

    @pl.when(s_ref[0] != 0)
    def _():
        m2_ref[:, 512:1280] = dqkv_ref[:, 0:768]


def feats_kernel(dqkv_ref, wqkv_ref, nx_ref, inv_ref, gain_ref, og_ref, out_ref, gg_ref, ys):
    ngrad = nt(dqkv_ref[...], wqkv_ref[...])
    nx = nx_ref[...]
    gg_ref[...] = jnp.sum(ngrad * nx, axis=0, keepdims=True)
    scaled = ngrad * gain_ref[...]
    correction = scaled - jnp.mean(scaled, axis=-1, keepdims=True) - nx * jnp.mean(scaled * nx, axis=-1, keepdims=True)
    ys[...] = inv_ref[:, 0:1] * correction
    for t in range(3):
        for r in range(7):
            out_ref[t, r] = (og_ref[t, r].astype(F32) + ys[t * 64 + r * 8 : t * 64 + r * 8 + 7, :]).astype(BF)


def put_small(write, bias, gain_rows):
    high = bias.astype(BF)
    write(slice(0, 256), high)
    write(slice(256, 512), (bias - high.astype(F32)).astype(BF))
    high = gain_rows.astype(BF)
    write(slice(512, 640), high)
    write(slice(640, 768), (gain_rows - high.astype(F32)).astype(BF))
    write(slice(768, 1024), jnp.zeros((8, 256), BF))


def get_small(block):
    return block[:, 0:256] + block[:, 256:512], block[:, 512:640] + block[:, 640:768]


def put_parts(refs, source, start, tall, bias, gain_rows):
    count = len(refs)
    for k in range(count):
        first = pl.multiple_of((start + k) % count * tall, tall)
        refs[k][0:tall] = source[pl.ds(first, tall), :].astype(BF)

        def write(lanes, value, k=k):
            refs[k][tall : tall + 8, lanes] = value

        put_small(write, bias, gain_rows)


def weights_kernel(s_ref, m1_own_ref, att_ref, dqkv_ref, ogk_ref, m1_ref, m2_ref, gg_ref, bias_ref, *refs):
    outs, (zs, gs) = refs[:-2], refs[-2:]
    tall = 1024 // len(outs)
    normed = m1_own_ref[:, 0:1024]

    @pl.when(s_ref[0] == 0)
    def _():
        zs[:, 0:768] = tn(normed, dqkv_ref[:, 0:768]) + tn(m1_ref[:, 0:1024], m2_ref[:, 512:1280])

    @pl.when(s_ref[0] != 0)
    def _():
        zs[:, 0:768] = tn(normed, dqkv_ref[:, 768:1536]) + tn(m1_ref[:, 0:1024], m2_ref[:, 512:1280])

    proj = tn(att_ref[...].reshape(192, 512), ogk_ref[...]) + tn(m2_ref[:, 0:512], m1_ref[:, 1024:1536])
    zs[0:512, 768:1024] = proj[:, 0:256]
    zs[512:1024, 768:1024] = proj[:, 256:512]
    for j in range(8):
        gs[j : j + 1, :] = gg_ref[:, j * 128 : j * 128 + 128]
    put_parts(outs, zs, s_ref[6], tall, bias_ref[...], gs[...])


def added(refs):
    total = refs[0][...].astype(F32)
    for ref in refs[1:]:
        total = total + ref[...].astype(F32)
    return total


def axis_sum_kernel(s_ref, *refs):
    count = (len(refs) - 1) // 2
    outs, total = refs[count : 2 * count], refs[2 * count]
    total[...] = added(refs[:count])
    tall = outs[0].shape[0] - 8
    bias, gain_rows = get_small(total[count * tall : count * tall + 8, :])
    put_parts(outs, total, s_ref[7], tall, bias, gain_rows)


def first_sum_kernel(*refs):
    out_ref = refs[-1]
    total = added(refs[:-1])
    groups, tall = out_ref.shape[:2]
    bias, gain_rows = get_small(total[groups * tall : groups * tall + 8])
    small = jnp.concatenate([bias[:, 0:128], bias[:, 128:256], gain_rows, jnp.zeros((8, 128), F32)], axis=0)
    share = 32 // groups
    zeros = jnp.zeros((tall - 2 * share, 128), F32) if tall > 2 * share else None
    for j in range(groups):
        out_ref[j, :, 0:1024] = total[j * tall : j * tall + tall].astype(BF)
        part = small[j * share : j * share + share]
        high = part.astype(BF).astype(F32)
        pieces = [high, part - high] + ([] if zeros is None else [zeros])
        out_ref[j, :, 1024:1152] = jnp.concatenate(pieces, axis=0).astype(BF)


def second_sum_kernel(y_ref, out_ref):
    count = y_ref.shape[0]
    total = y_ref[0].astype(F32)
    for i in range(1, count):
        total = total + y_ref[i].astype(F32)
    groups, tall = out_ref.shape[:2]
    share = 32 // groups
    main = total[:, 0:1024].astype(BF)
    part = total[0:share, 1024:1152] + total[share : 2 * share, 1024:1152]
    high = part.astype(BF).astype(F32)
    pieces = [high, part - high] + ([jnp.zeros((tall - 2 * share, 128), F32)] if tall > 2 * share else [])
    side = jnp.concatenate(pieces, axis=0).astype(BF)
    for j in range(groups):
        out_ref[j, :, 0:1024] = main
        out_ref[j, :, 1024:1152] = side


def spread_kernel(y_ref, out_ref, small_ref):
    groups, tall = y_ref.shape[:2]
    small_ref[...] = y_ref[:, :, 1024:1152]
    for j in range(groups):
        out_ref[j * tall : j * tall + tall] = y_ref[j, :, 0:1024]


def gather_kernel(s_ref, *refs):
    out_ref = refs[-1]
    count = len(refs) - 1
    tall = out_ref.shape[0] // count
    for k in range(count):
        first = pl.multiple_of((s_ref[7] + count - k) % count * tall, tall)
        out_ref[pl.ds(first, tall), :] = refs[k][...]


def small_kernel(small_ref, other_ref, out_ref):
    groups = small_ref.shape[0]
    share = 32 // groups
    for j in range(groups):
        both = small_ref[j].astype(F32) + other_ref[j].astype(F32)
        out_ref[j * share : j * share + share, :] = both[0:share] + both[share : 2 * share]


def place_kernel(blocks, count):
    def kernel(s_ref, *refs):
        sems = refs[-1]
        qkv_ref, proj_ref = refs[-3], refs[-2]

        def each(act):
            for n, (other, k) in enumerate(blocks):
                ref = refs[n]
                tall = ref.shape[0]
                start = s_ref[7] if other else s_ref[6]
                block = (start + count - k) % count
                first = pl.multiple_of(block * tall, tall)
                inner = pl.multiple_of(block * tall % 512, tall)
                for c in range(2):
                    mine = s_ref[0] == (1 - c if other else c)

                    @pl.when(mine)
                    def _(n=n, c=c, ref=ref, first=first):
                        act(pltpu.make_async_copy(ref.at[:, 0:768], qkv_ref.at[pl.ds(first, tall), c * 768 : c * 768 + 768], sems.at[2 * n]))

                    for half in range(2):

                        @pl.when(mine & (first // 512 == half))
                        def _(n=n, c=c, ref=ref, inner=inner, half=half):
                            lanes = slice(c * 512 + half * 256, c * 512 + half * 256 + 256)
                            act(pltpu.make_async_copy(ref.at[:, 768:1024], proj_ref.at[pl.ds(inner, tall), lanes], sems.at[2 * n + 1]))

        each(lambda copy: copy.start())
        each(lambda copy: copy.wait())

    return kernel


def call(kernel, outs, args, scratch=(), name=None, left=(), sems=0, outs_left=(), aliases=None, grant=24, pinned=()):
    def spec(i, a):
        space = pltpu.SMEM if a.dtype == jnp.int32 and a.ndim == 1 else pltpu.HBM if i in left else pltpu.VMEM
        return pl.BlockSpec(memory_space=space)

    specs = [spec(i, a) for i, a in enumerate(args)]
    args = [pltpu.with_memory_space_constraint(a, pltpu.HBM) if i in left and not INTERPRET else a for i, a in enumerate(args)]
    return pl.pallas_call(
        kernel,
        out_shape=[pltpu.HBM(shape, kind) if (i in pinned or i in outs_left) and not INTERPRET else jax.ShapeDtypeStruct(shape, kind) for i, (shape, kind) in enumerate(outs)],
        in_specs=specs,
        out_specs=[pl.BlockSpec(memory_space=pltpu.HBM if i in outs_left else pltpu.VMEM) for i in range(len(outs))],
        input_output_aliases=aliases or {},
        scratch_shapes=[pltpu.VMEM(shape, kind) for shape, kind in scratch] + ([pltpu.SemaphoreType.DMA((sems,))] if sems else []),
        compiler_params=pltpu.CompilerParams(vmem_limit_bytes=grant * 1024 * 1024),
        interpret=INTERPRET,
        name=name,
    )(*args)


def make_body(sizes):
    zl, nx_, zh, ny, nc = sizes
    rows, cols = zl * nx_, zh * ny * nc
    every = ("zl", "x", "zh", "y", "c")
    deep = zl * zh
    ids = np.arange(rows * cols).reshape(sizes)
    along_x = [[[int(v) for v in ids[a, :, b, k, c]] for a in range(zl) for b in range(zh) for k in range(ny)] for c in range(nc)]
    along_y = [[[int(v) for v in ids[a, k, b, :, c]] for a in range(zl) for b in range(zh) for k in range(nx_)] for c in range(nc)]
    first_groups = along_x[0] + along_y[1]
    second_groups = along_y[0] + along_x[1]
    assert nx_ == ny and nc == 2

    def row_pairs(value, first):
        pairs = []
        for low in range(first, rows - 1, 2):
            for j in range(cols):
                pairs += [(low * cols + j, (low + 1) * cols + j), ((low + 1) * cols + j, low * cols + j)]
        return lax.ppermute(value, every, pairs)

    def col_pairs(value, first):
        pairs = []
        for low in range(first, cols - 1, 2):
            for i in range(rows):
                pairs += [(i * cols + low, i * cols + low + 1), (i * cols + low + 1, i * cols + low)]
        return lax.ppermute(value, every, pairs)

    order = [0, 1, 3, 2] if nx_ == 4 else list(range(nx_))

    def onward(value, groups, k):
        return lax.ppermute(value, every, [(g[i], g[(i + k) % nx_]) for g in groups for i in range(nx_)])

    def parts_home(parts, groups):
        return [parts[0]] + [onward(parts[k], groups, k) for k in order[1:]]

    def from_all(value, groups):
        return {k: value if k == 0 else onward(value, groups, k) for k in order}

    def trade_deep(value):
        return lax.all_to_all(value, ("zl", "zh"), 0, 0, tiled=True)

    def swap(value):
        return lax.ppermute(value, "c", [(0, 1), (1, 0)])

    def body(image_feats, norm_gain, w_qkv, rel_bias, w_proj, out_grad):
        core = lax.axis_index("c")
        x_at = lax.axis_index("x")
        y_at = lax.axis_index("y")
        row_anchor = (lax.axis_index("zl") * nx_ + lax.axis_index("x")) * 7
        col_anchor = ((lax.axis_index("zh") * ny + lax.axis_index("y")) * nc + core) * 7
        scalars = jnp.stack([core, row_anchor, col_anchor, jnp.int32(rows * 7), jnp.int32(cols * 7), (row_anchor // 7) % 2, jnp.where(core == 0, x_at, y_at), jnp.where(core == 0, y_at, x_at)]).astype(jnp.int32)
        gain = norm_gain.reshape(1, 1024)
        pick = jnp.asarray(PICK, BF)
        perm = jnp.asarray(PERM, BF)
        rel = jnp.pad(rel_bias, ((0, 0), (0, 3), (0, 3))).reshape(8, 256)
        queries, own_kv, attn_grad, m1, og_keep, normal_x, inv_std, row_a, row_b = call(
            front_kernel,
            [((3, 64, 512), BF), ((3, 64, 1024), BF), ((3, 64, 512), BF), ((192, 1536), BF), ((192, 512), BF), ((192, 1024), F32), ((192, 128), F32), ((3, 24, 1024), BF), ((3, 24, 1024), BF)],
            [scalars, image_feats, out_grad, gain, w_qkv, w_proj],
            [((192, 1024), F32), ((192, 1024), F32), ((3, 7, 7, 1024), BF), ((3, 7, 7, 1024), BF), ((1, 1024), F32), ((1024, 1536), BF), ((512, 1024), BF), ((192, 1536), BF), ((192, 1024), F32)],
            "front",
            (1, 2, 3, 4, 5),
            8,
            (3, 5),
            pinned=(4, 6),
        )
        row_b = row_pairs(row_b, 1)
        row_a = row_pairs(row_a, 0)
        (table,) = call(
            table_kernel,
            [((512, 256), F32)],
            [scalars, rel, jnp.asarray(KEY_ROW), jnp.asarray(KEY_COL), perm],
            [((2, 512, 128), F32)],
            "table",
        )
        edges, col_a, col_b = call(
            columns_kernel,
            [((3, 64, 1024), BF), ((3, 40, 1024), BF), ((3, 40, 1024), BF)],
            [scalars, own_kv, row_a, row_b, pick],
            [((3, 128, 1024), BF)],
            "columns",
        )
        col_b = col_pairs(col_b, 1)
        col_a = col_pairs(col_a, 0)
        attended, query_grad, own_grad, col_a, col_b, score_sum = call(
            attention_kernel,
            [((3, 64, 512), BF), ((3, 64, 512), BF), ((3, 128, 1024), F32), ((3, 40, 1024), BF), ((3, 40, 1024), BF), ((512, 256), F32)],
            [scalars, queries, own_kv, edges, col_a, col_b, attn_grad, table],
            [((3, 256, 1024), BF), ((3, 96, 1024), BF)],
            "attention",
        )
        col_b = col_pairs(col_b, 1)
        col_a = col_pairs(col_a, 0)
        m1_other = swap(m1)
        layer_out, bias_part = call(
            out_kernel,
            [((3, 7, 7, 1024), BF), ((8, 256), F32)],
            [attended, w_proj, image_feats, score_sum, perm],
            [((192, 1024), F32), ((2, 512, 128), F32)],
            "layer_out",
        )
        own_sum, row_a, row_b = call(
            edges_kernel,
            [((3, 64, 1024), F32), ((3, 24, 1024), BF), ((3, 24, 1024), BF)],
            [scalars, own_grad, pick, col_a, col_b, bias_part],
            [((3, 96, 1024), BF)],
            "edges",
        )
        row_b = row_pairs(row_b, 1)
        row_a = row_pairs(row_a, 0)
        dqkv, m2 = call(
            join_kernel,
            [((192, 1536), BF), ((192, 1280), BF)],
            [scalars, own_sum, query_grad, attended, row_a, row_b, bias_part],
            [((3, 64, 1024), F32)],
            "join",
        )
        m2_other = swap(m2)
        feats_grad, gain_part = call(
            feats_kernel,
            [((3, 7, 7, 1024), BF), ((1, 1024), F32)],
            [dqkv, w_qkv, normal_x, inv_std, gain, out_grad],
            [((192, 1024), F32)],
            "feats",
        )
        tall1 = 1024 // nx_
        tall2 = tall1 // ny
        tall3 = tall2 // deep
        parts = call(
            weights_kernel,
            [((tall1 + 8, 1024), BF)] * nx_,
            [scalars, m1, attended, dqkv, og_keep, m1_other, m2_other, gain_part, bias_part],
            [((1024, 1024), F32), ((8, 128), F32)],
            "weights",
        )
        parts = parts_home(parts, first_groups)
        parts = call(axis_sum_kernel, [((tall2 + 8, 1024), BF)] * ny, [scalars] + parts, [((tall1 + 8, 1024), F32)], "first_sum")
        parts = parts_home(parts, second_groups)
        (send,) = call(first_sum_kernel, [((deep, tall3, 1152), BF)], parts, (), "second_sum")
        send = trade_deep(send)
        (send,) = call(second_sum_kernel, [((deep, tall3, 1152), BF)], [send], (), "third_sum")
        send = trade_deep(send)
        send, small = call(spread_kernel, [((tall2, 1024), BF), ((deep, tall3, 128), BF)], [send], (), "spread")
        small_other = swap(small)
        got = from_all(send, second_groups)
        (send,) = call(gather_kernel, [((tall1, 1024), BF)], [scalars] + [got[k] for k in range(ny)], (), "gather")
        send, small_other = lax.optimization_barrier((send, small_other))
        mine = from_all(send, first_groups)
        theirs = {k: swap(mine[k]) for k in order}
        (small,) = call(small_kernel, [((32, 128), F32)], [small, small_other], (), "small")
        grads = []
        for n, blocks in enumerate(([(0, k) for k in order[:-1]], [(0, order[-1])] + [(1, k) for k in order[:-1]], [(1, order[-1])])):
            count = len(blocks)
            grads = call(
                place_kernel(blocks, nx_),
                [((1024, 1536), BF), ((512, 1024), BF)],
                [scalars] + [theirs[k] if other else mine[k] for other, k in blocks] + list(grads),
                (),
                ("place_a", "place_b", "place_c")[n],
                (count + 1, count + 2) if n else (),
                2 * count,
                (0, 1),
                {count + 1: 0, count + 2: 1} if n else None,
            )
        qkv_grad, proj_grad = grads
        gain_grad = small[16:24].reshape(1024)
        bias_grad = jnp.concatenate([small[0:8], small[8:16]], axis=1).reshape(8, 16, 16)[:, :13, :13]
        return (layer_out, feats_grad, qkv_grad, proj_grad, gain_grad, bias_grad)

    return body


def solution(mesh, sizes=(2, 4, 4, 4, 2)):
    fine = Mesh(mesh.devices.reshape(sizes), ("zl", "x", "zh", "y", "c"))
    image = P(None, ("zl", "x"), ("zh", "y", "c"), None)
    return jax.shard_map(
        make_body(sizes),
        mesh=fine,
        in_specs=(image, P(), P(), P(), P(), image),
        out_specs=(image, image, P(), P(), P(), P()),
        check_vma=False,
    )
```
